128 devices in a mesh: seq: 16 (over x, y), enc: 8 (over z, core).
Axes of the slice: x: 4, y: 4, z: 4, core: 2. Of those that a mesh axis runs over, the one named last changes fastest.
Arguments:
- queries: bfloat16 [2048, 8192], P('seq', 'enc'), may hold values from -63 to 63
- image_key_value: bfloat16 [2, 128, 1601, 1024], P(None, ('seq', 'enc')), may hold values from -16 to 16
- image_spans: int32 [32, 2], replicated, may hold values from 0 to 2048, as said below
- tile_counts: int32 [32], replicated, may hold values from 1 to 4
- cross_gate: float32 [1], replicated, may hold values from 0.2 to 2
- grad_out: bfloat16 [2048, 8192], P('seq', 'enc'), may hold values from -6 to 6
Outputs:
- attended: bfloat16 [2048, 8192], P('seq', 'enc')
- grad_queries: bfloat16 [2048, 8192], P('seq', 'enc')
- grad_image_kv: bfloat16 [2, 128, 1601, 1024], P(None, ('seq', 'enc'))
The draws below stay inside these ranges and needn't reach their ends.
Inputs may be any that keep to these rules, and one draw needn't show every extreme that they name: `image_spans`: image m owns tiles 4 m to 4 m + 3. Its span starts in text shard m // 2 (positions (m // 2) * 128 to (m // 2) * 128 + 127), starts do not fall from one image to the next within a shard, and each span holds 1 to 128 positions.
All inputs are finite; a program needn't handle non-finite values.
Results may differ from the reference program's by a relative error of at most 0.0062.
Values may be sent and summed in bfloat16 or wider, within the bound.
A program may use at most 128 MiB of HBM per device.

```python
import jax
import jax.numpy as jnp
from jax import lax

QUERY_HEAD_COUNT = 64
KEY_VALUE_HEADS = 8
HEAD_SIZE = 128
TOKENS_PER_TILE = 1601
TILES = 4
TEXT_PER_SHARD = 128
TEXT = 2048
TILE_COUNT = 128
NIMG = 32
IMG_ROW = 2
N_SEQ = 16
N_ENC = 8


def span_table(key):
    base = jax.random.fold_in(key, 101)
    start_key, length_key = jax.random.split(base)
    offsets = jax.random.randint(start_key, (NIMG,), 0, TEXT_PER_SHARD)
    offsets = jnp.sort(offsets.reshape(NIMG // IMG_ROW, IMG_ROW), axis=1).reshape(NIMG)
    row_ids = jnp.arange(NIMG, dtype=jnp.int32) // IMG_ROW
    starts = row_ids * TEXT_PER_SHARD + offsets
    starts = starts.at[0].set(0)
    lengths = jax.random.randint(length_key, (NIMG,), 1, TEXT_PER_SHARD + 1)
    lengths = lengths.at[1].set(TEXT_PER_SHARD)
    span_ends = jnp.minimum(starts + lengths, TEXT)
    span_ends = span_ends.at[NIMG - 1].set(TEXT)
    return jnp.stack([starts, span_ends], 1).astype(jnp.int32)


def draw_image_spans(key, part):
    return span_table(key)


def draw_tile_counts(key, part):
    counts = jax.random.randint(jax.random.fold_in(key, 202), (NIMG,), 1, TILES + 1)
    return counts.at[0].set(TILES).astype(jnp.int32)


def draw_queries(key, part):
    base = jax.random.fold_in(key, 303)
    values = 2.0 * jnp.clip(jax.random.normal(base, (TEXT, QUERY_HEAD_COUNT * HEAD_SIZE), jnp.float32), -4.0, 4.0)
    return values.astype(jnp.bfloat16)


def draw_image_key_value(key, part):
    leading_key, trailing_key = jax.random.split(jax.random.fold_in(key, 404))
    key_portion = jnp.clip(jax.random.normal(leading_key, (TILE_COUNT, TOKENS_PER_TILE, KEY_VALUE_HEADS * HEAD_SIZE), jnp.float32), -4.0, 4.0)
    value_portion = 4.0 * jnp.clip(jax.random.normal(trailing_key, (TILE_COUNT, TOKENS_PER_TILE, KEY_VALUE_HEADS * HEAD_SIZE), jnp.float32), -4.0, 4.0)
    return jnp.stack([key_portion, value_portion], 0).astype(jnp.bfloat16)


def level_of(own_key, shape, pieces, least, high):
    def one(axis_at, blocks):
        draws = jax.random.uniform(jax.random.fold_in(jax.random.fold_in(own_key, 6), axis_at), (blocks,), jnp.float32, least / len(pieces), high / len(pieces))
        return jnp.repeat(jnp.exp(draws), shape[axis_at] // blocks).reshape((-1,) + (1,) * (len(shape) - axis_at - 1))

    loudness = one(*pieces[0])
    for cut in pieces[1:]:
        loudness = loudness * one(*cut)
    return loudness


def bell_draw(stream_key, extent, spread, most, cuts=(), held_as=jnp.bfloat16):
    entries = jax.random.normal(stream_key, extent, jnp.float32) * spread
    if len(cuts) > 0:
        entries = level_of(stream_key, extent, cuts, -0.22, 0.18) * entries
    return jnp.clip(entries, min=-most, max=most).astype(held_as)


def setup_inputs(seed: int = 0) -> dict:
    key_of = jax.random.split(jax.random.key(seed), 7)
    return {
        "queries": draw_queries(jax.random.fold_in(key_of[6], 71), 0),
        "image_key_value": draw_image_key_value(jax.random.fold_in(key_of[6], 71), 0),
        "image_spans": draw_image_spans(jax.random.fold_in(key_of[6], 71), 0),
        "tile_counts": draw_tile_counts(jax.random.fold_in(key_of[6], 71), 0),
        "cross_gate": jnp.clip(jax.random.uniform(key_of[4], (1,), jnp.float32, 0.2, 2.0), 0.2, 2.0),
        "grad_out": bell_draw(key_of[5], (TEXT, QUERY_HEAD_COUNT * HEAD_SIZE), 1.0, 6.0, ((0, 16), (1, 8))),
    }


NEG_FILL = -1.0e30


def visible_rows(image_spans, tile_counts, first_tile, tile_total, first_text, text_rows):
    image_total = image_spans.shape[0]
    tile_ids = first_tile + jnp.arange(tile_total, dtype=jnp.int32)
    image_ids = jnp.floor_divide(tile_ids, TILES)
    slot_ids = tile_ids - image_ids * TILES
    lookup = (image_ids[:, None] == jnp.arange(image_total, dtype=jnp.int32)[None, :]).astype(jnp.int32)
    starts = jnp.sum(lookup * image_spans[:, 0][None, :], axis=1)
    span_ends = jnp.sum(lookup * image_spans[:, 1][None, :], axis=1)
    in_use = jnp.sum(lookup * tile_counts[None, :], axis=1)
    usable = (tile_ids >= 0) & (slot_ids < in_use)
    positions = first_text + jnp.arange(text_rows, dtype=jnp.int32)
    return usable[None, :] & (positions[:, None] >= starts[None, :]) & (positions[:, None] < span_ends[None, :])


def head_terms(query_head, grad_head, key_head, value_head, visible, softmax_scale):
    query_wide = query_head.astype(jnp.float32)
    grad_wide = grad_head.astype(jnp.float32)
    key_wide = key_head.astype(jnp.float32)
    value_wide = value_head.astype(jnp.float32)
    text_rows = query_head.shape[0]
    head_groups = query_head.shape[1]
    head_dim = query_head.shape[2]
    tile_total = visible.shape[1]
    scores = jnp.einsum("tgd,jd->tgj", query_wide, key_wide) * softmax_scale
    tile_scores = jnp.moveaxis(scores.reshape(text_rows, head_groups, tile_total, TOKENS_PER_TILE), 2, 0)
    tile_values = value_wide.reshape(tile_total, TOKENS_PER_TILE, head_dim)

    def online(carried, item):
        tile_score, column, value_tile = item
        run_max, run_total, run_out = carried
        tile_mask = column[:, None, None]
        tile_max = jnp.max(jnp.where(tile_mask, tile_score, NEG_FILL), axis=2)
        new_max = jnp.maximum(run_max, tile_max)
        factor = jnp.exp(run_max - new_max)
        probs = jnp.where(tile_mask, jnp.exp(tile_score - new_max[:, :, None]), 0.0)
        probs_low = lax.optimization_barrier(probs.astype(jnp.bfloat16)).astype(jnp.float32)
        new_total = run_total * factor + jnp.sum(probs, axis=2)
        new_out = run_out * factor[:, :, None] + jnp.einsum("tgj,jd->tgd", probs_low, value_tile)
        return (new_max, new_total, new_out), None

    starting_state = (jnp.full((text_rows, head_groups), NEG_FILL, jnp.float32), jnp.zeros((text_rows, head_groups), jnp.float32),
               jnp.zeros((text_rows, head_groups, head_dim), jnp.float32))
    (run_max, run_total, run_out), unused = lax.scan(online, starting_state, (tile_scores, visible.T, tile_values))
    seen = run_total > 0.0
    safe_total = jnp.where(seen, run_total, 1.0)
    log_total = jnp.where(seen, run_max + jnp.log(safe_total), 0.0)
    mixed = jnp.where(seen[:, :, None], run_out / safe_total[:, :, None], 0.0)
    row_mask = jnp.repeat(visible, TOKENS_PER_TILE, axis=1)
    wide_mask = row_mask[:, None, :]
    weights = jnp.where(wide_mask, jnp.exp(scores - log_total[:, :, None]), 0.0)
    weights_low = lax.optimization_barrier(weights.astype(jnp.bfloat16)).astype(jnp.float32)
    row_delta = jnp.sum(grad_wide * mixed, axis=2)
    grad_weights = jnp.einsum("tgd,jd->tgj", grad_wide, value_wide)
    grad_scores = lax.optimization_barrier((weights * (grad_weights - row_delta[:, :, None])).astype(jnp.bfloat16)).astype(jnp.float32)
    query_grad = jnp.einsum("tgj,jd->tgd", grad_scores, key_wide) * softmax_scale
    key_grad = (jnp.einsum("tgj,tgd->jd", grad_scores, query_wide) * softmax_scale).astype(jnp.bfloat16)
    value_grad = jnp.einsum("tgj,tgd->jd", weights_low, grad_wide).astype(jnp.bfloat16)
    return mixed, query_grad, key_grad, value_grad


def reference(queries, image_key_value, image_spans, tile_counts, cross_gate, grad_out):
    softmax_scale = HEAD_SIZE ** -0.5
    head_groups = QUERY_HEAD_COUNT // KEY_VALUE_HEADS
    tile_row_block = N_ENC * TOKENS_PER_TILE
    gate_value = jnp.tanh(cross_gate[0])
    gradient_blended = (gate_value * grad_out.astype(jnp.float32)).astype(jnp.bfloat16)
    key_row_block = image_key_value[0].reshape(N_SEQ, tile_row_block, KEY_VALUE_HEADS, HEAD_SIZE)
    value_row_block = image_key_value[1].reshape(N_SEQ, tile_row_block, KEY_VALUE_HEADS, HEAD_SIZE)
    query_row_block = queries.reshape(N_SEQ, TEXT_PER_SHARD, KEY_VALUE_HEADS, head_groups, HEAD_SIZE)
    gradient_row_block = gradient_blended.reshape(N_SEQ, TEXT_PER_SHARD, KEY_VALUE_HEADS, head_groups, HEAD_SIZE)

    def row_step(carried, row_index):
        earlier = jnp.maximum(row_index - 1, 0)
        reach_keys = jnp.concatenate([key_row_block[earlier], key_row_block[row_index]], 0)
        reach_values = jnp.concatenate([value_row_block[earlier], value_row_block[row_index]], 0)
        visible = visible_rows(image_spans, tile_counts, (row_index - 1) * N_ENC, 2 * N_ENC, row_index * TEXT_PER_SHARD, TEXT_PER_SHARD)

        def one_head(head_items):
            query_head, grad_head, key_head, value_head = head_items
            return head_terms(query_head, grad_head, key_head, value_head, visible, softmax_scale)

        mixed, query_grad, key_grad, value_grad = lax.map(
            one_head,
            (jnp.moveaxis(query_row_block[row_index], 1, 0), jnp.moveaxis(gradient_row_block[row_index], 1, 0),
             jnp.moveaxis(reach_keys, 1, 0), jnp.moveaxis(reach_values, 1, 0)))
        finished_keys = (carried[0].astype(jnp.float32) + key_grad[:, :tile_row_block].astype(jnp.float32)).astype(jnp.bfloat16)
        finished_values = (carried[1].astype(jnp.float32) + value_grad[:, :tile_row_block].astype(jnp.float32)).astype(jnp.bfloat16)
        attended_rows = (gate_value * mixed).astype(jnp.bfloat16)
        return (key_grad[:, tile_row_block:], value_grad[:, tile_row_block:]), (attended_rows, query_grad.astype(jnp.bfloat16), finished_keys, finished_values)

    starting_state = (jnp.zeros((KEY_VALUE_HEADS, tile_row_block, HEAD_SIZE), jnp.bfloat16), jnp.zeros((KEY_VALUE_HEADS, tile_row_block, HEAD_SIZE), jnp.bfloat16))
    last_rows, stacked = lax.scan(row_step, starting_state, jnp.arange(N_SEQ, dtype=jnp.int32))
    attended = jnp.transpose(stacked[0], (0, 2, 1, 3, 4)).reshape(N_SEQ * TEXT_PER_SHARD, QUERY_HEAD_COUNT * HEAD_SIZE)
    grad_queries = jnp.transpose(stacked[1], (0, 2, 1, 3, 4)).reshape(N_SEQ * TEXT_PER_SHARD, QUERY_HEAD_COUNT * HEAD_SIZE)

    def assemble(shifted, final_row):
        entire_result = jnp.concatenate([shifted[1:], final_row[None]], 0)
        entire_result = entire_result.reshape(N_SEQ, KEY_VALUE_HEADS, N_ENC, TOKENS_PER_TILE, HEAD_SIZE)
        return jnp.transpose(entire_result, (0, 2, 3, 1, 4)).reshape(N_SEQ * N_ENC, TOKENS_PER_TILE, KEY_VALUE_HEADS * HEAD_SIZE)

    grad_image_kv = jnp.stack([assemble(stacked[2], last_rows[0]), assemble(stacked[3], last_rows[1])], 0)
    return attended, grad_queries, grad_image_kv
```

```python
import functools

import jax
import jax.numpy as jnp
from jax import lax
from jax.experimental import pallas as pl
from jax.experimental.pallas import tpu as pltpu
from jax.sharding import PartitionSpec as P

HEAD = 128
SLOTS = 128
TILES = 4
GROUP = 8
ROWS = GROUP * SLOTS
NEG = -1e30
LOG2E = 1.4426950408889634
SCALE = HEAD**-0.5
NT = (((1,), (1,)), ((), ()))
NN = (((1,), (0,)), ((), ()))
BF = jnp.bfloat16
F32 = jnp.float32


def dot(a, b, dims=NN):
    return lax.dot_general(a, b, dims, preferred_element_type=F32)


def chunks(keys, size):
    padded = -(-keys // 128) * 128
    return padded, [(o, min(size, padded - o)) for o in range(0, padded, size)]


def head_rows(block):
    return jnp.concatenate([block[:, h * HEAD : (h + 1) * HEAD] for h in range(GROUP)], 0)


def split_tile(keys, kv_block, wide, k_pad, v_pad):
    padded = k_pad.shape[0]
    wide[0 : 2 * keys, :] = kv_block.reshape(2 * keys, HEAD).astype(F32)
    wide[2 * keys :, :] = jnp.zeros((2 * (padded - keys), HEAD), F32)
    k_pad[...] = wide[pl.ds(0, padded, 2), :].astype(BF)
    v_pad[...] = wide[pl.ds(1, padded, 2), :].astype(BF)


def forward_group(keys, k_pad, v_t, q, probs, scores, out_t):
    padded, parts = chunks(keys, 256)
    top = jnp.full((8, ROWS), NEG, F32)
    for o, n in parts:
        s = dot(k_pad[o : o + n, :], q, NT)
        if o + n > keys:
            s = jnp.where(lax.broadcasted_iota(jnp.int32, s.shape, 0) < keys - o, s, NEG)
        scores[o : o + n, :] = s
        top = jnp.maximum(top, jnp.max(s.reshape(n // 8, 8, ROWS), axis=0))
    top = jnp.max(top, axis=0, keepdims=True) * (SCALE * LOG2E)
    total = jnp.zeros((8, ROWS), F32)
    acc = jnp.zeros((HEAD, ROWS), F32)
    for o, n in parts:
        p = jnp.exp2(scores[o : o + n, :] * (SCALE * LOG2E) - top)
        total = total + jnp.sum(p.reshape(n // 8, 8, ROWS), axis=0)
        low = p.astype(BF)
        probs[o : o + n, :] = low
        acc = acc + dot(v_t[:, o : o + n], low)
    total = jnp.sum(total, axis=0, keepdims=True)
    out_t[...] = acc / total
    return top, top + jnp.log2(total)


def backward_group(keys, v_pad, k_t, q, g, probs, factor, delta, dq_t, wide):
    padded, parts = chunks(keys, 256)
    for o, n in parts:
        dp = dot(v_pad[o : o + n, :], g, NT)
        p = probs[o : o + n, :].astype(F32) * factor
        t = (p * (dp - delta)).astype(BF)
        wide[pl.ds(2 * o, n, 2), :] = dot(t, q) * SCALE
        wide[pl.ds(2 * o + 1, n, 2), :] = dot(p.astype(BF), g)
        d = dot(k_t[:, o : o + n], t)
        dq_t[...] = d if o == 0 else dq_t[...] + d


def forward_kernel(keys, q_ref, g_ref, kv_ref, p_ref, o_ref, stat_ref, wide, k_pad, v_pad, v_t, scores):
    split_tile(keys, kv_ref[...], wide, k_pad, v_pad)
    v_t[...] = v_pad[...].T
    top, lse = forward_group(keys, k_pad, v_t, head_rows(q_ref[...]), p_ref, scores, o_ref)
    for h in range(GROUP):
        lanes = slice(h * SLOTS, (h + 1) * SLOTS)
        g_t = g_ref[:, h * HEAD : (h + 1) * HEAD].T.astype(F32)
        stat_ref[0, h : h + 1, :] = top[:, lanes]
        stat_ref[1, h : h + 1, :] = lse[:, lanes]
        stat_ref[2, h : h + 1, :] = jnp.sum(o_ref[:, lanes] * g_t, axis=0, keepdims=True)


def backward_kernel(
    keys, q_ref, g_ref, kv_ref, p_ref, o_ref, stat_ref, out_ref, dkv_ref, wide, k_pad, v_pad, k_t, dq_t
):
    split_tile(keys, kv_ref[...], wide, k_pad, v_pad)
    k_t[...] = k_pad[...].T

    def lanes_of(i):
        return jnp.concatenate([stat_ref[i, h : h + 1, :] for h in range(GROUP)], 1)

    backward_group(
        keys,
        v_pad,
        k_t,
        head_rows(q_ref[...]),
        head_rows(g_ref[...]),
        p_ref,
        lanes_of(0),
        lanes_of(2),
        dq_t,
        wide,
    )
    dkv_ref[...] = wide[0 : 2 * keys, :].astype(BF).reshape(keys, 2, HEAD)
    share = lanes_of(1)
    for h in range(GROUP):
        lanes = slice(h * SLOTS, (h + 1) * SLOTS)
        cols = slice(h * HEAD, (h + 1) * HEAD)
        out_ref[0, :, cols] = (o_ref[:, lanes] * share[:, lanes]).T.astype(BF)
        out_ref[1, :, cols] = (dq_t[:, lanes] * SCALE).T.astype(BF)


def per_group(*shape):
    return pl.BlockSpec((None,) + shape, lambda g: (g,) + (0,) * len(shape))


def kv_spec(keys):
    return pl.BlockSpec((keys, None, 2, HEAD), lambda g: (0, g, 0, 0))


def run_forward(q, g, kv):
    keys = kv.shape[0]
    padded = chunks(keys, 256)[0]
    groups = kv.shape[1]
    return pl.pallas_call(
        functools.partial(forward_kernel, keys),
        grid=(groups,),
        out_shape=[
            jax.ShapeDtypeStruct((groups, padded, ROWS), BF),
            jax.ShapeDtypeStruct((groups, HEAD, ROWS), F32),
            jax.ShapeDtypeStruct((groups, 3, GROUP, SLOTS), F32),
        ],
        in_specs=[per_group(SLOTS, GROUP * HEAD)] * 2 + [kv_spec(keys)],
        out_specs=[per_group(padded, ROWS), per_group(HEAD, ROWS), per_group(3, GROUP, SLOTS)],
        scratch_shapes=[
            pltpu.VMEM((2 * padded, HEAD), F32),
            pltpu.VMEM((padded, HEAD), BF),
            pltpu.VMEM((padded, HEAD), BF),
            pltpu.VMEM((HEAD, padded), BF),
            pltpu.VMEM((padded, ROWS), F32),
        ],
        compiler_params=pltpu.CompilerParams(vmem_limit_bytes=48 * 2**20),
    )(q, g, kv)


def run_backward(q, g, kv, probs, out_t, stats):
    keys, groups = kv.shape[:2]
    padded = probs.shape[1]
    return pl.pallas_call(
        functools.partial(backward_kernel, keys),
        grid=(groups,),
        out_shape=[
            jax.ShapeDtypeStruct((groups, 2, SLOTS, GROUP * HEAD), BF),
            jax.ShapeDtypeStruct(kv.shape, BF),
        ],
        in_specs=[per_group(SLOTS, GROUP * HEAD)] * 2
        + [kv_spec(keys), per_group(padded, ROWS), per_group(HEAD, ROWS), per_group(3, GROUP, SLOTS)],
        out_specs=[per_group(2, SLOTS, GROUP * HEAD), kv_spec(keys)],
        scratch_shapes=[
            pltpu.VMEM((2 * padded, HEAD), F32),
            pltpu.VMEM((padded, HEAD), BF),
            pltpu.VMEM((padded, HEAD), BF),
            pltpu.VMEM((HEAD, padded), BF),
            pltpu.VMEM((HEAD, ROWS), F32),
        ],
        compiler_params=pltpu.CompilerParams(vmem_limit_bytes=48 * 2**20),
    )(q, g, kv, probs, out_t, stats)


def shifted(x, by):
    n = lax.axis_size("seq")
    return lax.ppermute(x, "seq", [(i, (i + by) % n) for i in range(n)])


def exchange(x):
    return lax.all_to_all(x, "enc", split_axis=0, concat_axis=0, tiled=True)


def slot_masks(spans, counts, row, groups):
    tiles = row * groups + jnp.arange(groups, dtype=jnp.int32)
    images = tiles // TILES
    used = (tiles - images * TILES) < counts[images]
    start, end = spans[images, 0], spans[images, 1]
    own = row * SLOTS + jnp.arange(SLOTS, dtype=jnp.int32)[None, :]
    later = own + SLOTS
    here = used[:, None] & (own >= start[:, None]) & (own < end[:, None])
    after = used[:, None] & (later >= start[:, None]) & (later < end[:, None])
    return here, after


def shards(queries, image_key_value, image_spans, tile_counts, cross_gate, grad_out):
    row = lax.axis_index("seq")
    tile = lax.axis_index("enc")
    rows, groups = lax.axis_size("seq"), lax.axis_size("enc")
    keys = image_key_value.shape[2]
    gate = jnp.tanh(cross_gate[0])
    grads = (gate * grad_out.astype(F32)).astype(BF)
    kv = image_key_value.reshape(2, keys, groups, HEAD).transpose(1, 2, 0, 3)

    images = row * (groups // TILES) + jnp.arange(groups // TILES, dtype=jnp.int32)
    starts = image_spans[images, 0]
    own = (row * SLOTS + jnp.arange(SLOTS, dtype=jnp.int32))[None, :] >= starts[:, None]

    def gathered(x):
        y = jnp.where(own[:, :, None], x[None], shifted(x, -1)[None])
        return exchange(jnp.repeat(y, TILES, axis=0))

    q_all, g_all = gathered(queries), gathered(grads)
    probs, out_t, stats = run_forward(q_all, g_all, kv)

    here, after = slot_masks(image_spans, tile_counts, row, groups)
    here_before, after_before = slot_masks(image_spans, tile_counts, (row - 1) % rows, groups)
    here_next, after_next = slot_masks(image_spans, tile_counts, (row + 1) % rows, groups)
    mine = exchange(stats[:, 1:])
    before, later = shifted(mine, 1), shifted(mine, -1)

    def combined(a, a_mask, b, b_mask):
        lse = jnp.concatenate([a[:, 0], b[:, 0]], 0)
        lse = jnp.where(jnp.concatenate([a_mask, b_mask], 0)[:, None, :], lse, NEG)
        delta = jnp.concatenate([a[:, 1], b[:, 1]], 0)
        top = jnp.max(lse, axis=0)
        part = jnp.exp2(lse - top)
        part = jnp.where(lse > 0.5 * NEG, part, 0.0)
        total = jnp.sum(part, axis=0)
        safe = jnp.where(total > 0.0, total, 1.0)
        return top + jnp.log2(safe), jnp.sum(part * delta, axis=0) / safe

    lse_here, delta_here = combined(mine, here, before, after_before)
    lse_after, delta_after = combined(later, here_next, mine, after)
    pick = own[:, None, :]
    final = jnp.stack(
        [jnp.where(pick, lse_here, lse_after), jnp.where(pick, delta_here, delta_after)], 1
    )
    final = exchange(jnp.repeat(final, TILES, axis=0))
    valid = (here | after)[tile][None, None, :]
    factor = jnp.where(valid, jnp.exp2(stats[:, 0] - final[:, 0]), 0.0)
    share = jnp.where(valid, jnp.exp2(stats[:, 1] - final[:, 0]), 0.0)
    parts, dkv = run_backward(
        q_all, g_all, kv, probs, out_t, jnp.stack([factor, share, final[:, 1]], 1)
    )
    parts = exchange(parts).astype(F32)
    sums = parts.reshape(groups // TILES, TILES, 2, SLOTS, GROUP * HEAD).sum(1)
    at_own = own[:, None, :, None]
    stay = jnp.where(at_own, sums, 0.0).sum(0)
    leave = jnp.where(at_own, 0.0, sums).sum(0).astype(BF)
    total = stay + shifted(leave, 1).astype(F32)
    attended = (gate * total[0]).astype(BF)
    grad_queries = total[1].astype(BF)
    grad_image_kv = dkv.transpose(2, 0, 1, 3).reshape(2, 1, keys, groups * HEAD)
    return attended, grad_queries, grad_image_kv


def solution(mesh):
    kv_part = P(None, ("seq", "enc"), None, None)
    return jax.shard_map(
        shards,
        mesh=mesh,
        in_specs=(P("seq", "enc"), kv_part, P(), P(), P(), P("seq", "enc")),
        out_specs=(P("seq", "enc"), P("seq", "enc"), kv_part),
        check_vma=False,
    )
```

```python
import functools

import jax
import jax.numpy as jnp
from jax import lax
from jax.experimental import pallas as pl
from jax.experimental.pallas import tpu as pltpu
from jax.sharding import PartitionSpec as P

HEAD = 128
SLOTS = 128
TILES = 4
GROUP = 8
ROWS = GROUP * SLOTS
NEG = -1e30
LOG2E = 1.4426950408889634
SCALE = HEAD**-0.5
NT = (((1,), (1,)), ((), ()))
NN = (((1,), (0,)), ((), ()))
BF = jnp.bfloat16
F32 = jnp.float32


def dot(a, b, dims=NN):
    return lax.dot_general(a, b, dims, preferred_element_type=F32)


def chunks(keys, size):
    padded = -(-keys // 128) * 128
    return padded, [(o, min(size, padded - o)) for o in range(0, padded, size)]


def head_rows(block):
    return jnp.concatenate([block[:, h * HEAD : (h + 1) * HEAD] for h in range(GROUP)], 0)


def split_tile(keys, kv_block, wide, k_pad, v_pad):
    padded = k_pad.shape[0]
    wide[0 : 2 * keys, :] = kv_block.reshape(2 * keys, HEAD).astype(F32)
    wide[2 * keys :, :] = jnp.zeros((2 * (padded - keys), HEAD), F32)
    k_pad[...] = wide[pl.ds(0, padded, 2), :].astype(BF)
    v_pad[...] = wide[pl.ds(1, padded, 2), :].astype(BF)


def forward_group(keys, k_pad, v_t, q, probs, scores, out_t):
    padded, parts = chunks(keys, 256)
    top = jnp.full((8, ROWS), NEG, F32)
    for o, n in parts:
        s = dot(k_pad[o : o + n, :], q, NT)
        if o + n > keys:
            s = jnp.where(lax.broadcasted_iota(jnp.int32, s.shape, 0) < keys - o, s, NEG)
        scores[o : o + n, :] = s
        top = jnp.maximum(top, jnp.max(s.reshape(n // 8, 8, ROWS), axis=0))
    top = jnp.max(top, axis=0, keepdims=True) * (SCALE * LOG2E)
    total = jnp.zeros((8, ROWS), F32)
    acc = jnp.zeros((HEAD, ROWS), F32)
    for o, n in parts:
        p = jnp.exp2(scores[o : o + n, :] * (SCALE * LOG2E) - top)
        total = total + jnp.sum(p.reshape(n // 8, 8, ROWS), axis=0)
        low = p.astype(BF)
        probs[o : o + n, :] = low
        acc = acc + dot(v_t[:, o : o + n], low)
    total = jnp.sum(total, axis=0, keepdims=True)
    out_t[...] = acc / total
    return top, top + jnp.log2(total)


def backward_group(keys, v_pad, k_t, q, g, probs, factor, delta, dq_t, wide):
    padded, parts = chunks(keys, 256)
    for o, n in parts:
        dp = dot(v_pad[o : o + n, :], g, NT)
        p = probs[o : o + n, :].astype(F32) * factor
        t = (p * (dp - delta)).astype(BF)
        wide[pl.ds(2 * o, n, 2), :] = dot(t, q) * SCALE
        wide[pl.ds(2 * o + 1, n, 2), :] = dot(p.astype(BF), g)
        d = dot(k_t[:, o : o + n], t)
        dq_t[...] = d if o == 0 else dq_t[...] + d


MESH = pl.DeviceIdType.MESH


def merged(entries):
    top = entries[0][0]
    for lse, _ in entries[1:]:
        top = jnp.maximum(top, lse)
    total = jnp.zeros_like(top)
    mean = jnp.zeros_like(top)
    for lse, delta in entries:
        part = jnp.where(lse > 0.5 * NEG, jnp.exp2(lse - top), 0.0)
        total = total + part
        mean = mean + part * delta
    seen = total > 0.0
    safe = jnp.where(seen, total, 1.0)
    return jnp.where(seen, top + jnp.log2(safe), NEG), mean / safe


def step_kernel(
    keys,
    q_ref,
    g_ref,
    kv_ref,
    spans,
    counts,
    gate_ref,
    attended_ref,
    dq_ref,
    dkv_ref,
    g_low,
    next_q,
    next_g,
    pick_q,
    pick_g,
    q_all,
    g_all,
    kv_buf,
    dkv_buf,
    wide,
    k_pad,
    v_pad,
    turned,
    scores,
    probs,
    out_t,
    dq_t,
    tops,
    stat_out,
    stat_in,
    seq_out,
    seq_in,
    fin_out,
    fin_in,
    weight,
    o_out,
    o_in,
    d_out,
    d_in,
    stay,
    leave,
    arrived,
    kv_sem,
    dkv_sem,
    next_send,
    next_recv,
    q_send,
    q_recv,
    g_send,
    g_recv,
    stat_send,
    stat_recv,
    seq_send,
    seq_recv,
    fin_send,
    fin_recv,
    o_send,
    o_recv,
    d_send,
    d_recv,
    leave_send,
    leave_recv,
):
    row = lax.axis_index("seq")
    me = lax.axis_index("enc")
    rows = lax.axis_size("seq")
    groups = lax.axis_size("enc")
    chips = groups // 2
    z, core = me // 2, me % 2
    other = me + 1 - 2 * core
    image = me // TILES
    above, below = (row + 1) % rows, (row + rows - 1) % rows

    def remote(src, dst, send, recv, to):
        return pltpu.make_async_remote_copy(
            src_ref=src, dst_ref=dst, send_sem=send, recv_sem=recv, device_id=to, device_id_type=MESH
        )

    def group_at(i):
        j = i // 2
        hop = j + j // 2 - 2 * (j // 3)
        return 2 * ((z + hop) % chips) + (core + i) % 2

    def kv_load(g, slot):
        return pltpu.make_async_copy(kv_ref.at[:, g], kv_buf.at[slot, 0:keys], kv_sem.at[slot])

    def dkv_store(g, slot):
        return pltpu.make_async_copy(dkv_buf.at[slot, 0:keys], dkv_ref.at[:, g], dkv_sem.at[slot])

    kv_load(group_at(0), 0).start()

    barrier = pltpu.get_barrier_semaphore()
    for j in range(1, groups):
        pl.semaphore_signal(barrier, inc=1, device_id=(row, (me + j) % groups), device_id_type=MESH)
    for r in (above, below):
        pl.semaphore_signal(barrier, inc=1, device_id=(r, me), device_id_type=MESH)
    pl.semaphore_wait(barrier, groups + 1)

    to_below = (below, me)
    send_q = remote(q_ref, next_q, next_send.at[0], next_recv.at[0], to_below)
    send_q.start()
    gate = jnp.tanh(jnp.full((SLOTS, HEAD), gate_ref[0], F32))
    for h in range(GROUP):
        cols = slice(h * HEAD, (h + 1) * HEAD)
        g_low[:, cols] = (gate * g_ref[:, cols].astype(F32)).astype(BF)
    send_g = remote(g_low, next_g, next_send.at[1], next_recv.at[1], to_below)
    send_g.start()

    starts = [spans[2 * row + i, 0] for i in range(2)]
    ends = [spans[2 * row + i, 1] for i in range(2)]
    used = [counts[2 * row + i] for i in range(2)]
    at_rows = row * SLOTS + lax.broadcasted_iota(jnp.int32, (SLOTS, HEAD), 0)
    at_lanes = row * SLOTS + lax.broadcasted_iota(jnp.int32, (GROUP, SLOTS), 1)
    own_rows = [at_rows >= starts[i] for i in range(2)]
    own_lanes = [at_lanes >= starts[i] for i in range(2)]

    def fan_out(mine, later, picked, everywhere, send, recv):
        for h in range(GROUP):
            cols = slice(h * HEAD, (h + 1) * HEAD)
            a, b = mine[:, cols].astype(F32), later[:, cols].astype(F32)
            for i in range(2):
                picked[i, :, cols] = jnp.where(own_rows[i], a, b).astype(BF)
        everywhere[me] = picked[image]
        remote(picked.at[image], everywhere.at[me], send.at[0], recv.at[me], (row, other)).start()
        for n, hop in enumerate((1, chips - 1, 2)):
            peer = 2 * ((z + hop) % chips) + core
            remote(
                picked.at[peer // TILES], everywhere.at[me], send.at[1 + n], recv.at[me], (row, peer)
            ).start()

    def arrival(buf, send, recv, g):
        return remote(buf.at[g], buf.at[g], send.at[0], recv.at[g], (row, other))

    def hand_on(buf, send, recv, i, n):
        g = group_at(i)
        return remote(buf.at[g], buf.at[g], send.at[n], recv.at[g], (row, other))

    send_q.wait_recv()
    fan_out(q_ref, next_q, pick_q, q_all, q_send, q_recv)
    send_g.wait_recv()
    fan_out(g_low, next_g, pick_g, g_all, g_send, g_recv)

    def forward(i, carry):
        g = group_at(i)
        slot = i % 2
        kv_load(g, slot).wait()
        kv_load(group_at(jnp.minimum(i + 1, groups - 1)), 1 - slot).start()

        @pl.when(i > 0)
        def _():
            arrival(q_all, q_send, q_recv, g).wait_recv()

        for n in range(3):
            @pl.when(i == 2 + 2 * n)
            def _():
                hand_on(q_all, q_send, q_recv, 2 + 2 * n, 4 + n).start()

            @pl.when(i == 5 + n)
            def _():
                arrival(g_all, g_send, g_recv, group_at(2 + 2 * n)).wait_recv()
                hand_on(g_all, g_send, g_recv, 2 + 2 * n, 4 + n).start()

        split_tile(keys, kv_buf[slot, 0:keys], wide, k_pad, v_pad)
        turned[...] = v_pad[...].T
        top, lse = forward_group(
            keys, k_pad, turned, head_rows(q_all[g]), probs.at[g], scores, out_t.at[g]
        )
        for h in range(GROUP):
            lanes = slice(h * SLOTS, (h + 1) * SLOTS)
            tops[g, h : h + 1, :] = top[:, lanes]
            stat_out[g, 0, h : h + 1, :] = lse[:, lanes]
        return carry

    lax.fori_loop(0, groups, forward, 0)

    def stat_copy(g, n):
        return remote(stat_out.at[g], stat_in.at[me], stat_send.at[n], stat_recv.at[me], (row, g))

    def delta(i, carry):
        g = group_at(i)

        @pl.when(i % 2 == 1)
        def _():
            arrival(g_all, g_send, g_recv, g).wait_recv()

        for h in range(GROUP):
            lanes = slice(h * SLOTS, (h + 1) * SLOTS)
            g_t = g_all[g, :, h * HEAD : (h + 1) * HEAD].T.astype(F32)
            stat_out[g, 1, h : h + 1, :] = jnp.sum(out_t[g, :, lanes] * g_t, axis=0, keepdims=True)

        @pl.when(i > 0)
        def _():
            stat_copy(g, i).start()

        return carry

    lax.fori_loop(0, groups, delta, 0)
    stat_in[me] = stat_out[me]
    for j in range(1, groups):
        src = (me + j) % groups
        remote(stat_out.at[0], stat_in.at[src], stat_send.at[0], stat_recv.at[src], (row, src)).wait_recv()

    def seen(c, shift):
        i = c // TILES
        end = jnp.where(c % TILES < used[i], ends[i], 0)
        at = at_lanes + shift
        return (at >= starts[i]) & (at < end)

    here, after = [], []
    for c in range(2 * TILES):
        lse, mean = stat_in[c, 0], stat_in[c, 1]
        here.append((jnp.where(seen(c, 0), lse, NEG), mean))
        after.append((jnp.where(seen(c, SLOTS), lse, NEG), mean))
    here, after = merged(here), merged(after)
    seq_out[0, 0], seq_out[0, 1] = after
    seq_out[1, 0], seq_out[1, 1] = here
    up = remote(seq_out.at[0], seq_in.at[0], seq_send.at[0], seq_recv.at[0], (above, me))
    down = remote(seq_out.at[1], seq_in.at[1], seq_send.at[1], seq_recv.at[1], (below, me))
    up.start()
    down.start()
    up.wait_recv()
    down.wait_recv()
    here = merged([here, (seq_in[0, 0], seq_in[0, 1])])
    after = merged([after, (seq_in[1, 0], seq_in[1, 1])])
    for i in range(2):
        for n in range(2):
            fin_out[i, n] = jnp.where(own_lanes[i], here[n], after[n])
    fin_in[me] = fin_out[image]
    for j in range(1, groups):
        c = (me + j) % groups
        remote(fin_out.at[c // TILES], fin_in.at[me], fin_send.at[j], fin_recv.at[me], (row, c)).start()

    my_used = counts[2 * row + image]
    my_start = spans[2 * row + image, 0]
    my_end = jnp.where(me % TILES < my_used, spans[2 * row + image, 1], 0)
    shown = ((at_lanes >= my_start) & (at_lanes < my_end)) | (
        (at_lanes + SLOTS >= my_start) & (at_lanes + SLOTS < my_end)
    )

    def part_copy(out, dest, send, recv, g, n):
        return remote(out.at[g], dest.at[me], send.at[n], recv.at[me], (row, g))

    def settle(out, dest, recv, send, n, result):
        for j in range(1, groups):
            src = (me + j) % groups
            remote(out.at[0], dest.at[src], send.at[0], recv.at[src], (row, src)).wait_recv()
        dest[me] = out[me]
        for h in range(GROUP):
            cols = slice(h * HEAD, (h + 1) * HEAD)
            sums = []
            for i in range(2):
                total = dest[TILES * i, :, cols].astype(F32)
                for c in range(1, TILES):
                    total = total + dest[TILES * i + c, :, cols].astype(F32)
                sums.append(total)
            kept = [jnp.where(own_rows[i], sums[i], 0.0) for i in range(2)]
            gone = [jnp.where(own_rows[i], 0.0, sums[i]) for i in range(2)]
            stay[n, :, cols] = kept[0] + kept[1]
            leave[n, :, cols] = (gone[0] + gone[1]).astype(BF)
        leave_copy(n).start()

    def leave_copy(n):
        return remote(leave.at[n], arrived.at[n], leave_send.at[n], leave_recv.at[n], (above, me))

    def backward(i, carry):
        g = group_at(groups - 1 - i)
        slot = i % 2
        kv_load(g, slot).wait()

        @pl.when(i < groups - 1)
        def _():
            kv_load(group_at(groups - 2 - i), 1 - slot).start()
            remote(fin_out.at[0], fin_in.at[g], fin_send.at[0], fin_recv.at[g], (row, g)).wait_recv()

        lse, mean = fin_in[g, 0], fin_in[g, 1]
        weight[0] = jnp.where(shown, jnp.exp2(tops[g] - lse), 0.0)
        weight[1] = jnp.where(shown, jnp.exp2(stat_out[g, 0] - lse), 0.0)
        weight[2] = mean

        def lanes_of(n):
            return jnp.concatenate([weight[n, h : h + 1, :] for h in range(GROUP)], 1)

        for h in range(GROUP):
            lanes = slice(h * SLOTS, (h + 1) * SLOTS)
            cols = slice(h * HEAD, (h + 1) * HEAD)
            o_out[g, :, cols] = (out_t[g, :, lanes] * weight[1, h : h + 1, :]).T.astype(BF)

        @pl.when(i < groups - 1)
        def _():
            part_copy(o_out, o_in, o_send, o_recv, g, i).start()

        @pl.when(i == groups - 1)
        def _():
            settle(o_out, o_in, o_recv, o_send, 0, attended_ref)

        @pl.when(i >= 2)
        def _():
            dkv_store(g, slot).wait()

        split_tile(keys, kv_buf[slot, 0:keys], wide, k_pad, v_pad)
        turned[...] = k_pad[...].T
        backward_group(
            keys,
            v_pad,
            turned,
            head_rows(q_all[g]),
            head_rows(g_all[g]),
            probs.at[g],
            lanes_of(0),
            lanes_of(2),
            dq_t,
            wide,
        )
        for h in range(GROUP):
            lanes = slice(h * SLOTS, (h + 1) * SLOTS)
            cols = slice(h * HEAD, (h + 1) * HEAD)
            d_out[g, :, cols] = (dq_t[:, lanes] * SCALE).T.astype(BF)

        @pl.when(i < groups - 1)
        def _():
            part_copy(d_out, d_in, d_send, d_recv, g, i).start()

        dkv_buf[slot, 0:keys] = wide[0 : 2 * keys, :].astype(BF).reshape(keys, 2, HEAD)
        dkv_store(g, slot).start()
        return carry

    lax.fori_loop(0, groups, backward, 0)
    settle(d_out, d_in, d_recv, d_send, 1, dq_ref)

    for n, result in enumerate((attended_ref, dq_ref)):
        leave_copy(n).wait_recv()
        for h in range(GROUP):
            cols = slice(h * HEAD, (h + 1) * HEAD)
            total = stay[n, :, cols] + arrived[n, :, cols].astype(F32)
            result[:, cols] = (gate * total if n == 0 else total).astype(BF)

    send_q.wait_send()
    send_g.wait_send()
    for n in range(7):
        hand_on(q_all, q_send, q_recv, 2, n).wait_send()
        hand_on(g_all, g_send, g_recv, 2, n).wait_send()
    for n in range(1, groups):
        stat_copy(0, n).wait_send()
        remote(fin_out.at[0], fin_in.at[0], fin_send.at[n], fin_recv.at[0], (row, other)).wait_send()
        part_copy(o_out, o_in, o_send, o_recv, 0, n - 1).wait_send()
        part_copy(d_out, d_in, d_send, d_recv, 0, n - 1).wait_send()
    up.wait_send()
    down.wait_send()
    for n in range(2):
        leave_copy(n).wait_send()
        dkv_store(0, n).wait()


def shards(queries, image_key_value, image_spans, tile_counts, cross_gate, grad_out):
    groups = lax.axis_size("enc")
    keys = image_key_value.shape[2]
    padded = chunks(keys, 256)[0]
    kv = image_key_value.reshape(2, keys, groups, HEAD).transpose(1, 2, 0, 3)
    wide = GROUP * HEAD
    vmem = pl.BlockSpec(memory_space=pltpu.VMEM)
    smem = pl.BlockSpec(memory_space=pltpu.SMEM)
    anywhere = pl.BlockSpec(memory_space=pl.ANY)
    block = pltpu.VMEM((SLOTS, wide), BF)
    pair = pltpu.VMEM((2, SLOTS, wide), BF)
    every = pltpu.VMEM((groups, SLOTS, wide), BF)
    stats = pltpu.VMEM((groups, 2, GROUP, SLOTS), F32)
    two_stats = pltpu.VMEM((2, 2, GROUP, SLOTS), F32)
    text = jax.ShapeDtypeStruct((SLOTS, wide), BF)
    sems = [2, 2, 2, 2, 7, 8, 7, 8, 8, 8, 2, 2, 8, 8, 7, 8, 7, 8, 2, 2]
    attended, grad_queries, dkv = pl.pallas_call(
        functools.partial(step_kernel, keys),
        out_shape=[text, text, jax.ShapeDtypeStruct(kv.shape, BF)],
        in_specs=[vmem, vmem, anywhere, smem, smem, smem],
        out_specs=[vmem, vmem, anywhere],
        scratch_shapes=[
            block,
            block,
            block,
            pair,
            pair,
            every,
            every,
            pltpu.VMEM((2, padded, 2, HEAD), BF),
            pltpu.VMEM((2, padded, 2, HEAD), BF),
            pltpu.VMEM((2 * padded, HEAD), F32),
            pltpu.VMEM((padded, HEAD), BF),
            pltpu.VMEM((padded, HEAD), BF),
            pltpu.VMEM((HEAD, padded), BF),
            pltpu.VMEM((padded, ROWS), F32),
            pltpu.VMEM((groups, padded, ROWS), BF),
            pltpu.VMEM((groups, HEAD, ROWS), F32),
            pltpu.VMEM((HEAD, ROWS), F32),
            pltpu.VMEM((groups, GROUP, SLOTS), F32),
            stats,
            stats,
            two_stats,
            two_stats,
            two_stats,
            stats,
            pltpu.VMEM((3, GROUP, SLOTS), F32),
            every,
            every,
            every,
            every,
            pltpu.VMEM((2, SLOTS, wide), F32),
            pair,
            pair,
        ]
        + [pltpu.SemaphoreType.DMA((n,)) for n in sems],
        compiler_params=pltpu.CompilerParams(
            collective_id=0, has_side_effects=True, vmem_limit_bytes=63 * 2**20
        ),
    )(queries, grad_out, kv, image_spans, tile_counts, cross_gate)
    grad_image_kv = dkv.transpose(2, 0, 1, 3).reshape(2, 1, keys, groups * HEAD)
    return attended, grad_queries, grad_image_kv


def solution(mesh):
    kv_part = P(None, ("seq", "enc"), None, None)
    return jax.shard_map(
        shards,
        mesh=mesh,
        in_specs=(P("seq", "enc"), kv_part, P(), P(), P(), P("seq", "enc")),
        out_specs=(P("seq", "enc"), P("seq", "enc"), kv_part),
        check_vma=False,
    )
```

```python
import functools

import jax
import jax.numpy as jnp
from jax import lax
from jax.experimental import pallas as pl
from jax.experimental.pallas import tpu as pltpu
from jax.sharding import PartitionSpec as P

HEAD = 128
SLOTS = 128
TILES = 4
GROUP = 8
ROWS = GROUP * SLOTS
NEG = -1e30
LOG2E = 1.4426950408889634
SCALE = HEAD**-0.5
NT = (((1,), (1,)), ((), ()))
NN = (((1,), (0,)), ((), ()))
BF = jnp.bfloat16
F32 = jnp.float32


def dot(a, b, dims=NN):
    return lax.dot_general(a, b, dims, preferred_element_type=F32)


def chunks(keys, size):
    padded = -(-keys // 128) * 128
    return padded, [(o, min(size, padded - o)) for o in range(0, padded, size)]


def head_rows(block):
    return jnp.concatenate([block[:, h * HEAD : (h + 1) * HEAD] for h in range(GROUP)], 0)


def split_tile(keys, kv_block, wide, k_pad, v_pad):
    padded = k_pad.shape[0]
    wide[0 : 2 * keys, :] = kv_block.reshape(2 * keys, HEAD).astype(F32)
    wide[2 * keys :, :] = jnp.zeros((2 * (padded - keys), HEAD), F32)
    k_pad[...] = wide[pl.ds(0, padded, 2), :].astype(BF)
    v_pad[...] = wide[pl.ds(1, padded, 2), :].astype(BF)


def forward_group(keys, k_pad, v_t, q, probs, scores, out_t):
    padded, parts = chunks(keys, 256)
    top = jnp.full((8, ROWS), NEG, F32)
    for o, n in parts:
        s = dot(k_pad[o : o + n, :], q, NT)
        if o + n > keys:
            s = jnp.where(lax.broadcasted_iota(jnp.int32, s.shape, 0) < keys - o, s, NEG)
        scores[o : o + n, :] = s
        top = jnp.maximum(top, jnp.max(s.reshape(n // 8, 8, ROWS), axis=0))
    top = jnp.max(top, axis=0, keepdims=True) * (SCALE * LOG2E)
    total = jnp.zeros((8, ROWS), F32)
    acc = jnp.zeros((HEAD, ROWS), F32)
    for o, n in parts:
        p = jnp.exp2(scores[o : o + n, :] * (SCALE * LOG2E) - top)
        total = total + jnp.sum(p.reshape(n // 8, 8, ROWS), axis=0)
        low = p.astype(BF)
        probs[o : o + n, :] = low
        acc = acc + dot(v_t[:, o : o + n], low)
    total = jnp.sum(total, axis=0, keepdims=True)
    out_t[...] = acc / total
    return top, top + jnp.log2(total)


def backward_group(keys, v_pad, k_t, q, g, probs, factor, delta, dq_t, wide):
    padded, parts = chunks(keys, 256)
    for o, n in parts:
        dp = dot(v_pad[o : o + n, :], g, NT)
        p = probs[o : o + n, :].astype(F32) * factor
        t = (p * (dp - delta)).astype(BF)
        wide[pl.ds(2 * o, n, 2), :] = dot(t, q) * SCALE
        wide[pl.ds(2 * o + 1, n, 2), :] = dot(p.astype(BF), g)
        d = dot(k_t[:, o : o + n], t)
        dq_t[...] = d if o == 0 else dq_t[...] + d


MESH = pl.DeviceIdType.MESH
LAG = 3


def merged(entries):
    top = entries[0][0]
    for lse, _ in entries[1:]:
        top = jnp.maximum(top, lse)
    total = jnp.zeros_like(top)
    mean = jnp.zeros_like(top)
    for lse, delta in entries:
        part = jnp.where(lse > 0.5 * NEG, jnp.exp2(lse - top), 0.0)
        total = total + part
        mean = mean + part * delta
    seen = total > 0.0
    safe = jnp.where(seen, total, 1.0)
    return jnp.where(seen, top + jnp.log2(safe), NEG), mean / safe


def step_kernel(
    keys,
    q_hbm,
    g_hbm,
    kv_ref,
    spans,
    counts,
    gate_ref,
    attended_ref,
    dq_ref,
    dkv_ref,
    q_ref,
    g_ref,
    g_low,
    next_q,
    next_g,
    pick_q,
    pick_g,
    q_all,
    g_all,
    kv_buf,
    dkv_buf,
    wide,
    k_pad,
    v_pad,
    turned,
    scores,
    probs,
    out_t,
    dq_t,
    tops,
    stat_out,
    stat_in,
    seq_out,
    seq_in,
    fin_out,
    fin_in,
    weight,
    o_out,
    o_sib,
    o_in,
    d_out,
    d_sib,
    d_in,
    stay,
    leave,
    arrived,
    text_sem,
    kv_sem,
    dkv_sem,
    next_send,
    next_recv,
    q_send,
    q_recv,
    g_send,
    g_recv,
    stat_send,
    stat_recv,
    seq_send,
    seq_recv,
    fin_send,
    fin_recv,
    o_sib_send,
    o_sib_recv,
    o_send,
    o_recv,
    d_sib_send,
    d_sib_recv,
    d_send,
    d_recv,
    leave_send,
    leave_recv,
):
    row = lax.axis_index("seq")
    me = lax.axis_index("enc")
    rows = lax.axis_size("seq")
    groups = lax.axis_size("enc")
    chips = groups // 2
    z, core = me // 2, me % 2
    other = me + 1 - 2 * core
    image = me // TILES
    above, below = (row + 1) % rows, (row + rows - 1) % rows

    def remote(src, dst, send, recv, to):
        return pltpu.make_async_remote_copy(
            src_ref=src, dst_ref=dst, send_sem=send, recv_sem=recv, device_id=to, device_id_type=MESH
        )

    def group_at(i):
        j = i // 2
        hop = j + j // 2 - 2 * (j // 3)
        return 2 * ((z + hop) % chips) + (core + i) % 2

    def kv_load(g, slot):
        return pltpu.make_async_copy(kv_ref.at[:, g], kv_buf.at[slot, 0:keys], kv_sem.at[slot])

    def dkv_store(g, slot):
        return pltpu.make_async_copy(dkv_buf.at[slot, 0:keys], dkv_ref.at[:, g], dkv_sem.at[slot])

    text = [
        pltpu.make_async_copy(q_hbm, q_ref, text_sem.at[0]),
        pltpu.make_async_copy(g_hbm, g_ref, text_sem.at[1]),
    ]
    for copy in text:
        copy.start()
    kv_load(group_at(0), 0).start()

    barrier = pltpu.get_barrier_semaphore()
    for j in range(1, groups):
        pl.semaphore_signal(barrier, inc=1, device_id=(row, (me + j) % groups), device_id_type=MESH)
    for r in (above, below):
        pl.semaphore_signal(barrier, inc=1, device_id=(r, me), device_id_type=MESH)
    pl.semaphore_wait(barrier, groups + 1)

    to_below = (below, me)
    text[0].wait()
    send_q = remote(q_ref, next_q, next_send.at[0], next_recv.at[0], to_below)
    send_q.start()
    text[1].wait()
    gate = jnp.tanh(jnp.full((SLOTS, HEAD), gate_ref[0], F32))
    for h in range(GROUP):
        cols = slice(h * HEAD, (h + 1) * HEAD)
        g_low[:, cols] = (gate * g_ref[:, cols].astype(F32)).astype(BF)
    send_g = remote(g_low, next_g, next_send.at[1], next_recv.at[1], to_below)
    send_g.start()

    starts = [spans[0, 2 * row + i] for i in range(2)]
    ends = [spans[1, 2 * row + i] for i in range(2)]
    used = [counts[2 * row + i] for i in range(2)]
    at_rows = row * SLOTS + lax.broadcasted_iota(jnp.int32, (SLOTS, HEAD), 0)
    at_lanes = row * SLOTS + lax.broadcasted_iota(jnp.int32, (GROUP, SLOTS), 1)
    own_rows = [at_rows >= starts[i] for i in range(2)]
    own_lanes = [at_lanes >= starts[i] for i in range(2)]

    def fan_out(mine, later, picked, everywhere, send, recv):
        for h in range(GROUP):
            cols = slice(h * HEAD, (h + 1) * HEAD)
            a, b = mine[:, cols].astype(F32), later[:, cols].astype(F32)
            for i in range(2):
                picked[i, :, cols] = jnp.where(own_rows[i], a, b).astype(BF)
        everywhere[me] = picked[image]
        remote(picked.at[image], everywhere.at[me], send.at[0], recv.at[me], (row, other)).start()
        for n, hop in enumerate((1, chips - 1, 2)):
            peer = 2 * ((z + hop) % chips) + core
            remote(
                picked.at[peer // TILES], everywhere.at[me], send.at[1 + n], recv.at[me], (row, peer)
            ).start()

    def arrival(buf, send, recv, g):
        return remote(buf.at[g], buf.at[g], send.at[0], recv.at[g], (row, other))

    def hand_on(buf, send, recv, i, n):
        g = group_at(i)
        return remote(buf.at[g], buf.at[g], send.at[n], recv.at[g], (row, other))

    send_q.wait_recv()
    fan_out(q_ref, next_q, pick_q, q_all, q_send, q_recv)

    def stat_copy(g, n):
        return remote(stat_out.at[g], stat_in.at[me], stat_send.at[n], stat_recv.at[me], (row, g))

    def delta(g):
        for h in range(GROUP):
            lanes = slice(h * SLOTS, (h + 1) * SLOTS)
            g_t = g_all[g, :, h * HEAD : (h + 1) * HEAD].T.astype(F32)
            stat_out[g, 1, h : h + 1, :] = jnp.sum(out_t[g, :, lanes] * g_t, axis=0, keepdims=True)

    def forward(i, carry):
        g = group_at(i)
        slot = i % 2
        kv_load(g, slot).wait()
        kv_load(group_at(jnp.minimum(i + 1, groups - 1)), 1 - slot).start()

        @pl.when(i > 0)
        def _():
            arrival(q_all, q_send, q_recv, g).wait_recv()

        @pl.when(i == 1)
        def _():
            send_g.wait_recv()
            fan_out(g_low, next_g, pick_g, g_all, g_send, g_recv)

        for n in range(3):

            @pl.when(i == 2 + 2 * n)
            def _():
                hand_on(q_all, q_send, q_recv, 2 + 2 * n, 4 + n).start()

            @pl.when(i == 5 + n)
            def _():
                arrival(g_all, g_send, g_recv, group_at(2 + 2 * n)).wait_recv()
                hand_on(g_all, g_send, g_recv, 2 + 2 * n, 4 + n).start()

        late = group_at(jnp.maximum(i - LAG, 0))

        @pl.when((i > LAG) & ((i - LAG) % 2 == 1))
        def _():
            arrival(g_all, g_send, g_recv, late).wait_recv()

        delta(late)

        @pl.when(i > LAG)
        def _():
            stat_copy(late, i - LAG).start()

        split_tile(keys, kv_buf[slot, 0:keys], wide, k_pad, v_pad)
        turned[...] = v_pad[...].T
        top, lse = forward_group(
            keys, k_pad, turned, head_rows(q_all[g]), probs.at[g], scores, out_t.at[g]
        )
        for h in range(GROUP):
            lanes = slice(h * SLOTS, (h + 1) * SLOTS)
            tops[g, h : h + 1, :] = top[:, lanes]
            stat_out[g, 0, h : h + 1, :] = lse[:, lanes]
        return carry

    lax.fori_loop(0, groups, forward, 0)

    for i in range(TILES * 2 - LAG, TILES * 2):
        late = group_at(i)
        if i % 2 == 1:
            arrival(g_all, g_send, g_recv, late).wait_recv()
        delta(late)
        stat_copy(late, i).start()
    stat_in[me] = stat_out[me]
    for j in range(1, groups):
        src = (me + j) % groups
        remote(stat_out.at[0], stat_in.at[src], stat_send.at[0], stat_recv.at[src], (row, src)).wait_recv()

    def seen(c, shift):
        i = c // TILES
        end = jnp.where(c % TILES < used[i], ends[i], 0)
        at = at_lanes + shift
        return (at >= starts[i]) & (at < end)

    here, after = [], []
    for c in range(2 * TILES):
        lse, mean = stat_in[c, 0], stat_in[c, 1]
        here.append((jnp.where(seen(c, 0), lse, NEG), mean))
        after.append((jnp.where(seen(c, SLOTS), lse, NEG), mean))
    here, after = merged(here), merged(after)
    seq_out[0, 0], seq_out[0, 1] = after
    seq_out[1, 0], seq_out[1, 1] = here
    up = remote(seq_out.at[0], seq_in.at[0], seq_send.at[0], seq_recv.at[0], (above, me))
    down = remote(seq_out.at[1], seq_in.at[1], seq_send.at[1], seq_recv.at[1], (below, me))
    up.start()
    down.start()
    up.wait_recv()
    down.wait_recv()
    here = merged([here, (seq_in[0, 0], seq_in[0, 1])])
    after = merged([after, (seq_in[1, 0], seq_in[1, 1])])
    for i in range(2):
        for n in range(2):
            fin_out[i, n] = jnp.where(own_lanes[i], here[n], after[n])
    fin_in[me] = fin_out[image]
    for j in range(1, groups):
        c = (me + j) % groups
        remote(fin_out.at[c // TILES], fin_in.at[me], fin_send.at[j], fin_recv.at[me], (row, c)).start()

    my_used = counts[2 * row + image]
    my_start = spans[0, 2 * row + image]
    my_end = jnp.where(me % TILES < my_used, spans[1, 2 * row + image], 0)
    shown = ((at_lanes >= my_start) & (at_lanes < my_end)) | (
        (at_lanes + SLOTS >= my_start) & (at_lanes + SLOTS < my_end)
    )

    def to_sibling(out, sib, send, recv, g, j):
        return remote(out.at[g], sib.at[j], send.at[j], recv.at[j], (row, other))

    def to_owner(out, dest, send, recv, g, j):
        return remote(out.at[g], dest.at[z], send.at[j], recv.at[z], (row, g))

    def pass_on(values, out, sib, dest, sib_send, sib_recv, send, recv, i, g):
        j = (groups - 1 - i) // 2

        @pl.when(i % 2 == 0)
        def _():
            for h in range(GROUP):
                out[g, :, h * HEAD : (h + 1) * HEAD] = values(h).astype(BF)
            to_sibling(out, sib, sib_send, sib_recv, g, j).start()

        @pl.when(i % 2 == 1)
        def _():
            to_sibling(out, sib, sib_send, sib_recv, g, j).wait_recv()
            for h in range(GROUP):
                cols = slice(h * HEAD, (h + 1) * HEAD)
                out[g, :, cols] = (values(h) + sib[j, :, cols].astype(F32)).astype(BF)

        @pl.when((i % 2 == 1) & (i < groups - 1))
        def _():
            to_owner(out, dest, send, recv, g, j).start()

    def settle(out, dest, recv, send, n):
        for j in range(1, chips):
            src = (z + j) % chips
            remote(out.at[0], dest.at[src], send.at[0], recv.at[src], (row, 2 * src + core)).wait_recv()
        dest[z] = out[me]
        for h in range(GROUP):
            cols = slice(h * HEAD, (h + 1) * HEAD)
            sums = []
            for i in range(2):
                sums.append(dest[2 * i, :, cols].astype(F32) + dest[2 * i + 1, :, cols].astype(F32))
            kept = [jnp.where(own_rows[i], sums[i], 0.0) for i in range(2)]
            gone = [jnp.where(own_rows[i], 0.0, sums[i]) for i in range(2)]
            stay[n, :, cols] = kept[0] + kept[1]
            leave[n, :, cols] = (gone[0] + gone[1]).astype(BF)
        leave_copy(n).start()

    def leave_copy(n):
        return remote(leave.at[n], arrived.at[n], leave_send.at[n], leave_recv.at[n], (above, me))

    def backward(i, carry):
        g = group_at(groups - 1 - i)
        slot = i % 2
        kv_load(g, slot).wait()

        @pl.when(i < groups - 1)
        def _():
            kv_load(group_at(groups - 2 - i), 1 - slot).start()
            remote(fin_out.at[0], fin_in.at[g], fin_send.at[0], fin_recv.at[g], (row, g)).wait_recv()

        lse, mean = fin_in[g, 0], fin_in[g, 1]
        weight[0] = jnp.where(shown, jnp.exp2(tops[g] - lse), 0.0)
        weight[1] = jnp.where(shown, jnp.exp2(stat_out[g, 0] - lse), 0.0)
        weight[2] = mean

        def lanes_of(n):
            return jnp.concatenate([weight[n, h : h + 1, :] for h in range(GROUP)], 1)

        def o_rows(h):
            return (out_t[g, :, h * SLOTS : (h + 1) * SLOTS] * weight[1, h : h + 1, :]).T

        pass_on(o_rows, o_out, o_sib, o_in, o_sib_send, o_sib_recv, o_send, o_recv, i, g)

        @pl.when(i == groups - 1)
        def _():
            settle(o_out, o_in, o_recv, o_send, 0)

        @pl.when(i >= 2)
        def _():
            dkv_store(g, slot).wait()

        split_tile(keys, kv_buf[slot, 0:keys], wide, k_pad, v_pad)
        turned[...] = k_pad[...].T
        backward_group(
            keys,
            v_pad,
            turned,
            head_rows(q_all[g]),
            head_rows(g_all[g]),
            probs.at[g],
            lanes_of(0),
            lanes_of(2),
            dq_t,
            wide,
        )
        def d_rows(h):
            return (dq_t[:, h * SLOTS : (h + 1) * SLOTS] * SCALE).T

        pass_on(d_rows, d_out, d_sib, d_in, d_sib_send, d_sib_recv, d_send, d_recv, i, g)
        dkv_buf[slot, 0:keys] = wide[0 : 2 * keys, :].astype(BF).reshape(keys, 2, HEAD)
        dkv_store(g, slot).start()
        return carry

    lax.fori_loop(0, groups, backward, 0)
    settle(d_out, d_in, d_recv, d_send, 1)

    for n, result in enumerate((attended_ref, dq_ref)):
        leave_copy(n).wait_recv()
        for h in range(GROUP):
            cols = slice(h * HEAD, (h + 1) * HEAD)
            total = stay[n, :, cols] + arrived[n, :, cols].astype(F32)
            result[:, cols] = (gate * total if n == 0 else total).astype(BF)

    send_q.wait_send()
    send_g.wait_send()
    for n in range(7):
        hand_on(q_all, q_send, q_recv, 2, n).wait_send()
        hand_on(g_all, g_send, g_recv, 2, n).wait_send()
    for n in range(1, groups):
        stat_copy(0, n).wait_send()
        remote(fin_out.at[0], fin_in.at[0], fin_send.at[n], fin_recv.at[0], (row, other)).wait_send()
    for j in range(chips):
        to_sibling(o_out, o_sib, o_sib_send, o_sib_recv, 0, j).wait_send()
        to_sibling(d_out, d_sib, d_sib_send, d_sib_recv, 0, j).wait_send()
    for j in range(1, chips):
        remote(o_out.at[0], o_in.at[0], o_send.at[j], o_recv.at[0], (row, other)).wait_send()
        remote(d_out.at[0], d_in.at[0], d_send.at[j], d_recv.at[0], (row, other)).wait_send()
    up.wait_send()
    down.wait_send()
    for n in range(2):
        leave_copy(n).wait_send()
        dkv_store(0, n).wait()


def finish_kernel(pieces, a_in, d_in, kv_in, a_out, d_out, kv_out, a_buf, d_buf, kv_buf, loads, stores):
    keys = kv_in.shape[0]
    step = -(-keys // pieces)
    parts = [slice(n * step, min((n + 1) * step, keys)) for n in range(pieces)]
    moves = [(a_in, a_buf, a_out), (d_in, d_buf, d_out)]
    moves += [(kv_in.at[p], kv_buf.at[p], kv_out.at[p]) for p in parts]
    into = [pltpu.make_async_copy(m[0], m[1], loads.at[n]) for n, m in enumerate(moves)]
    out = [pltpu.make_async_copy(m[1], m[2], stores.at[n]) for n, m in enumerate(moves)]
    for copy in into:
        copy.start()
    for copy, store in zip(into, out):
        copy.wait()
        store.start()
    for store in out:
        store.wait()


def shards(queries, image_key_value, image_spans, tile_counts, cross_gate, grad_out):
    groups = lax.axis_size("enc")
    keys = image_key_value.shape[2]
    padded = chunks(keys, 256)[0]
    kv = image_key_value.reshape(2, keys, groups, HEAD).transpose(1, 2, 0, 3)
    wide = GROUP * HEAD
    vmem = pl.BlockSpec(memory_space=pltpu.VMEM)
    smem = pl.BlockSpec(memory_space=pltpu.SMEM)
    anywhere = pl.BlockSpec(memory_space=pl.ANY)
    block = pltpu.VMEM((SLOTS, wide), BF)
    pair = pltpu.VMEM((2, SLOTS, wide), BF)
    every = pltpu.VMEM((groups, SLOTS, wide), BF)
    quarter = pltpu.VMEM((groups // 2, SLOTS, wide), BF)
    stats = pltpu.VMEM((groups, 2, GROUP, SLOTS), F32)
    two_stats = pltpu.VMEM((2, 2, GROUP, SLOTS), F32)
    text = jax.ShapeDtypeStruct((SLOTS, wide), BF)
    sems = [2, 2, 2, 2, 2, 7, 8, 7, 8, 8, 8, 2, 2, 8, 8] + [4] * 8 + [2, 2]
    attended, grad_queries, dkv = pl.pallas_call(
        functools.partial(step_kernel, keys),
        out_shape=[text, text, jax.ShapeDtypeStruct(kv.shape, BF)],
        in_specs=[anywhere, anywhere, anywhere, smem, smem, smem],
        out_specs=[vmem, vmem, anywhere],
        scratch_shapes=[
            block,
            block,
            block,
            block,
            block,
            pair,
            pair,
            every,
            every,
            pltpu.VMEM((2, padded, 2, HEAD), BF),
            pltpu.VMEM((2, padded, 2, HEAD), BF),
            pltpu.VMEM((2 * padded, HEAD), F32),
            pltpu.VMEM((padded, HEAD), BF),
            pltpu.VMEM((padded, HEAD), BF),
            pltpu.VMEM((HEAD, padded), BF),
            pltpu.VMEM((padded, ROWS), F32),
            pltpu.VMEM((groups, padded, ROWS), BF),
            pltpu.VMEM((groups, HEAD, ROWS), F32),
            pltpu.VMEM((HEAD, ROWS), F32),
            pltpu.VMEM((groups, GROUP, SLOTS), F32),
            stats,
            stats,
            two_stats,
            two_stats,
            two_stats,
            stats,
            pltpu.VMEM((3, GROUP, SLOTS), F32),
            every,
            quarter,
            quarter,
            every,
            quarter,
            quarter,
            pltpu.VMEM((2, SLOTS, wide), F32),
            pair,
            pair,
        ]
        + [pltpu.SemaphoreType.DMA((n,)) for n in sems],
        compiler_params=pltpu.CompilerParams(
            collective_id=0, has_side_effects=True, vmem_limit_bytes=63 * 2**20
        ),
    )(queries, grad_out, kv, image_spans.T, tile_counts, cross_gate)
    pieces = 16
    attended, grad_queries, dkv = pl.pallas_call(
        functools.partial(finish_kernel, pieces),
        out_shape=[text, text, jax.ShapeDtypeStruct(kv.shape, BF)],
        in_specs=[anywhere] * 3,
        out_specs=[anywhere] * 3,
        scratch_shapes=[block, block, pltpu.VMEM(kv.shape, BF)]
        + [pltpu.SemaphoreType.DMA((pieces + 2,))] * 2,
        compiler_params=pltpu.CompilerParams(vmem_limit_bytes=62 * 2**20),
    )(attended, grad_queries, dkv)
    grad_image_kv = dkv.transpose(2, 0, 1, 3).reshape(2, 1, keys, groups * HEAD)
    return attended, grad_queries, grad_image_kv


def solution(mesh):
    kv_part = P(None, ("seq", "enc"), None, None)
    return jax.shard_map(
        shards,
        mesh=mesh,
        in_specs=(P("seq", "enc"), kv_part, P(), P(), P(), P("seq", "enc")),
        out_specs=(P("seq", "enc"), P("seq", "enc"), kv_part),
        check_vma=False,
    )
```

```python
import functools

import jax
import jax.numpy as jnp
from jax import lax
from jax.experimental import pallas as pl
from jax.experimental.pallas import tpu as pltpu
from jax.sharding import PartitionSpec as P

HEAD = 128
SLOTS = 128
TILES = 4
GROUP = 8
ROWS = GROUP * SLOTS
NEG = -1e30
LOG2E = 1.4426950408889634
SCALE = HEAD**-0.5
NT = (((1,), (1,)), ((), ()))
NN = (((1,), (0,)), ((), ()))
BF = jnp.bfloat16
F32 = jnp.float32


def dot(a, b, dims=NN):
    return lax.dot_general(a, b, dims, preferred_element_type=F32)


def chunks(keys, size):
    padded = -(-keys // 128) * 128
    return padded, [(o, min(size, padded - o)) for o in range(0, padded, size)]


def head_rows(block):
    return jnp.concatenate([block[:, h * HEAD : (h + 1) * HEAD] for h in range(GROUP)], 0)


def split_tile(keys, kv_block, wide, k_pad, v_pad):
    padded = k_pad.shape[0]
    wide[0 : 2 * keys, :] = kv_block.reshape(2 * keys, HEAD).astype(F32)
    wide[2 * keys :, :] = jnp.zeros((2 * (padded - keys), HEAD), F32)
    k_pad[...] = wide[pl.ds(0, padded, 2), :].astype(BF)
    v_pad[...] = wide[pl.ds(1, padded, 2), :].astype(BF)


def forward_group(keys, k_pad, v_t, q, probs, scores, out_t):
    padded, parts = chunks(keys, 896)
    top = jnp.full((8, ROWS), NEG, F32)
    for o, n in parts:
        s = dot(k_pad[o : o + n, :], q, NT)
        if o + n > keys:
            s = jnp.where(lax.broadcasted_iota(jnp.int32, s.shape, 0) < keys - o, s, NEG)
        scores[o : o + n, :] = s
        top = jnp.maximum(top, jnp.max(s.reshape(n // 8, 8, ROWS), axis=0))
    top = jnp.max(top, axis=0, keepdims=True) * (SCALE * LOG2E)
    total = jnp.zeros((8, ROWS), F32)
    acc = jnp.zeros((HEAD, ROWS), F32)
    for o, n in parts:
        p = jnp.exp2(scores[o : o + n, :] * (SCALE * LOG2E) - top)
        total = total + jnp.sum(p.reshape(n // 8, 8, ROWS), axis=0)
        low = p.astype(BF)
        probs[o : o + n, :] = low
        acc = acc + dot(v_t[:, o : o + n], low)
    total = jnp.sum(total, axis=0, keepdims=True)
    out_t[...] = acc / total
    return top, top + jnp.log2(total)


def backward_group(keys, v_pad, k_t, q, g, probs, factor, delta, dq_t, wide):
    padded, parts = chunks(keys, 896)
    for o, n in parts:
        dp = dot(v_pad[o : o + n, :], g, NT)
        p = probs[o : o + n, :].astype(F32) * factor
        t = (p * (dp - delta)).astype(BF)
        wide[pl.ds(2 * o, n, 2), :] = dot(t, q) * SCALE
        wide[pl.ds(2 * o + 1, n, 2), :] = dot(p.astype(BF), g)
        d = dot(k_t[:, o : o + n], t)
        dq_t[...] = d if o == 0 else dq_t[...] + d


MESH = pl.DeviceIdType.MESH
LAG = 3
PIECE = 2


def merged(entries):
    top = entries[0][0]
    for lse, _ in entries[1:]:
        top = jnp.maximum(top, lse)
    total = jnp.zeros_like(top)
    mean = jnp.zeros_like(top)
    for lse, delta in entries:
        part = jnp.where(lse > 0.5 * NEG, jnp.exp2(lse - top), 0.0)
        total = total + part
        mean = mean + part * delta
    seen = total > 0.0
    safe = jnp.where(seen, total, 1.0)
    return jnp.where(seen, top + jnp.log2(safe), NEG), mean / safe


def step_kernel(
    keys,
    q_hbm,
    g_hbm,
    kv_ref,
    spans,
    counts,
    gate_ref,
    attended_ref,
    dq_ref,
    dkv_ref,
    q_ref,
    g_ref,
    g_low,
    next_q,
    next_g,
    pick_q,
    pick_g,
    q_all,
    g_all,
    kv_buf,
    dkv_buf,
    wide,
    k_pad,
    v_pad,
    turned,
    scores,
    probs,
    out_t,
    dq_t,
    tops,
    stat_out,
    stat_in,
    seq_out,
    seq_in,
    fin_out,
    fin_in,
    weight,
    o_out,
    o_sib,
    o_in,
    d_out,
    d_sib,
    d_in,
    stay,
    leave,
    arrived,
    text_sem,
    kv_sem,
    dkv_sem,
    next_send,
    next_recv,
    q_send,
    q_recv,
    g_send,
    g_recv,
    stat_send,
    stat_recv,
    seq_send,
    seq_recv,
    fin_send,
    fin_recv,
    o_sib_send,
    o_sib_recv,
    o_send,
    o_recv,
    d_sib_send,
    d_sib_recv,
    d_send,
    d_recv,
    leave_send,
    leave_recv,
):
    row = lax.axis_index("seq")
    me = lax.axis_index("enc")
    rows = lax.axis_size("seq")
    groups = lax.axis_size("enc")
    chips = groups // 2
    z, core = me // 2, me % 2
    other = me + 1 - 2 * core
    image = me // TILES
    above, below = (row + 1) % rows, (row + rows - 1) % rows

    def remote(src, dst, send, recv, to):
        return pltpu.make_async_remote_copy(
            src_ref=src, dst_ref=dst, send_sem=send, recv_sem=recv, device_id=to, device_id_type=MESH
        )

    def group_at(i):
        j = i // 2
        hop = j + j // 2 - 2 * (j // 3)
        return 2 * ((z + hop) % chips) + (core + i) % 2

    def kv_load(g, slot):
        return pltpu.make_async_copy(kv_ref.at[:, g], kv_buf.at[slot, 0:keys], kv_sem.at[slot])

    def dkv_store(g, slot):
        return pltpu.make_async_copy(dkv_buf.at[slot, 0:keys], dkv_ref.at[:, g], dkv_sem.at[slot])

    text = [
        pltpu.make_async_copy(q_hbm, q_ref, text_sem.at[0]),
        pltpu.make_async_copy(g_hbm, g_ref, text_sem.at[1]),
    ]
    for copy in text:
        copy.start()
    kv_load(group_at(0), 0).start()

    barrier = pltpu.get_barrier_semaphore()
    for j in range(1, groups):
        pl.semaphore_signal(barrier, inc=1, device_id=(row, (me + j) % groups), device_id_type=MESH)
    for r in (above, below):
        pl.semaphore_signal(barrier, inc=1, device_id=(r, me), device_id_type=MESH)
    pl.semaphore_wait(barrier, groups + 1)

    to_below = (below, me)
    text[0].wait()
    send_q = remote(q_ref, next_q, next_send.at[0], next_recv.at[0], to_below)
    send_q.start()
    text[1].wait()
    gate = jnp.tanh(jnp.full((SLOTS, HEAD), gate_ref[0], F32))
    for h in range(GROUP):
        cols = slice(h * HEAD, (h + 1) * HEAD)
        g_low[:, cols] = (gate * g_ref[:, cols].astype(F32)).astype(BF)
    send_g = remote(g_low, next_g, next_send.at[1], next_recv.at[1], to_below)
    send_g.start()

    starts = [spans[0, 2 * row + i] for i in range(2)]
    ends = [spans[1, 2 * row + i] for i in range(2)]
    used = [counts[2 * row + i] for i in range(2)]
    at_rows = row * SLOTS + lax.broadcasted_iota(jnp.int32, (SLOTS, HEAD), 0)
    at_lanes = row * SLOTS + lax.broadcasted_iota(jnp.int32, (GROUP, SLOTS), 1)
    own_rows = [at_rows >= starts[i] for i in range(2)]
    own_lanes = [at_lanes >= starts[i] for i in range(2)]

    def fan_out(mine, later, picked, everywhere, send, recv):
        for h in range(GROUP):
            cols = slice(h * HEAD, (h + 1) * HEAD)
            a, b = mine[:, cols].astype(F32), later[:, cols].astype(F32)
            for i in range(2):
                picked[i, :, cols] = jnp.where(own_rows[i], a, b).astype(BF)
        everywhere[me] = picked[image]
        remote(picked.at[image], everywhere.at[me], send.at[0], recv.at[me], (row, other)).start()
        for n, hop in enumerate((1, chips - 1, 2)):
            peer = 2 * ((z + hop) % chips) + core
            remote(
                picked.at[peer // TILES], everywhere.at[me], send.at[1 + n], recv.at[me], (row, peer)
            ).start()

    def arrival(buf, send, recv, g):
        return remote(buf.at[g], buf.at[g], send.at[0], recv.at[g], (row, other))

    def hand_on(buf, send, recv, i, n):
        g = group_at(i)
        return remote(buf.at[g], buf.at[g], send.at[n], recv.at[g], (row, other))

    send_q.wait_recv()
    fan_out(q_ref, next_q, pick_q, q_all, q_send, q_recv)

    def stat_copy(g, n):
        return remote(stat_out.at[g], stat_in.at[me], stat_send.at[n], stat_recv.at[me], (row, g))

    def delta(g):
        for h in range(GROUP):
            lanes = slice(h * SLOTS, (h + 1) * SLOTS)
            g_t = g_all[g, :, h * HEAD : (h + 1) * HEAD].T.astype(F32)
            stat_out[g, 1, h : h + 1, :] = jnp.sum(out_t[g, :, lanes] * g_t, axis=0, keepdims=True)

    def forward(i, carry):
        g = group_at(i)
        slot = i % 2
        kv_load(g, slot).wait()
        kv_load(group_at(jnp.minimum(i + 1, groups - 1)), 1 - slot).start()

        @pl.when(i > 0)
        def _():
            arrival(q_all, q_send, q_recv, g).wait_recv()

        @pl.when(i == 1)
        def _():
            send_g.wait_recv()
            fan_out(g_low, next_g, pick_g, g_all, g_send, g_recv)

        for n in range(3):

            @pl.when(i == 2 + 2 * n)
            def _():
                hand_on(q_all, q_send, q_recv, 2 + 2 * n, 4 + n).start()

            @pl.when(i == 5 + n)
            def _():
                arrival(g_all, g_send, g_recv, group_at(2 + 2 * n)).wait_recv()
                hand_on(g_all, g_send, g_recv, 2 + 2 * n, 4 + n).start()

        late = group_at(jnp.maximum(i - LAG, 0))

        @pl.when((i > LAG) & ((i - LAG) % 2 == 1))
        def _():
            arrival(g_all, g_send, g_recv, late).wait_recv()

        delta(late)

        @pl.when(i > LAG)
        def _():
            stat_copy(late, i - LAG).start()

        split_tile(keys, kv_buf[slot, 0:keys], wide, k_pad, v_pad)
        turned[...] = v_pad[...].T
        top, lse = forward_group(
            keys, k_pad, turned, head_rows(q_all[g]), probs.at[g], scores, out_t.at[g]
        )
        for h in range(GROUP):
            lanes = slice(h * SLOTS, (h + 1) * SLOTS)
            tops[g, h : h + 1, :] = top[:, lanes]
            stat_out[g, 0, h : h + 1, :] = lse[:, lanes]
        return carry

    lax.fori_loop(0, groups, forward, 0)

    for i in range(TILES * 2 - LAG, TILES * 2):
        late = group_at(i)
        if i % 2 == 1:
            arrival(g_all, g_send, g_recv, late).wait_recv()
        delta(late)
        stat_copy(late, i).start()
    stat_in[me] = stat_out[me]
    for j in range(1, groups):
        src = (me + j) % groups
        remote(stat_out.at[0], stat_in.at[src], stat_send.at[0], stat_recv.at[src], (row, src)).wait_recv()

    def seen(c, shift):
        i = c // TILES
        end = jnp.where(c % TILES < used[i], ends[i], 0)
        at = at_lanes + shift
        return (at >= starts[i]) & (at < end)

    here, after = [], []
    for c in range(2 * TILES):
        lse, mean = stat_in[c, 0], stat_in[c, 1]
        here.append((jnp.where(seen(c, 0), lse, NEG), mean))
        after.append((jnp.where(seen(c, SLOTS), lse, NEG), mean))
    here, after = merged(here), merged(after)
    seq_out[0, 0], seq_out[0, 1] = after
    seq_out[1, 0], seq_out[1, 1] = here
    up = remote(seq_out.at[0], seq_in.at[0], seq_send.at[0], seq_recv.at[0], (above, me))
    down = remote(seq_out.at[1], seq_in.at[1], seq_send.at[1], seq_recv.at[1], (below, me))
    up.start()
    down.start()
    up.wait_recv()
    down.wait_recv()
    here = merged([here, (seq_in[0, 0], seq_in[0, 1])])
    after = merged([after, (seq_in[1, 0], seq_in[1, 1])])
    for i in range(2):
        for n in range(2):
            fin_out[i, n] = jnp.where(own_lanes[i], here[n], after[n])
    fin_in[me] = fin_out[image]
    for j in range(1, groups):
        c = (me + j) % groups
        remote(fin_out.at[c // TILES], fin_in.at[me], fin_send.at[j], fin_recv.at[me], (row, c)).start()

    my_used = counts[2 * row + image]
    my_start = spans[0, 2 * row + image]
    my_end = jnp.where(me % TILES < my_used, spans[1, 2 * row + image], 0)
    shown = ((at_lanes >= my_start) & (at_lanes < my_end)) | (
        (at_lanes + SLOTS >= my_start) & (at_lanes + SLOTS < my_end)
    )

    def to_sibling(out, sib, send, recv, g, j):
        return remote(out.at[g], sib.at[j], send.at[j], recv.at[j], (row, other))

    def to_owner(out, dest, send, recv, g, j):
        return remote(out.at[g], dest.at[z], send.at[j], recv.at[z], (row, g))

    def pass_on(values, out, sib, dest, sib_send, sib_recv, send, recv, i, g):
        j = (groups - 1 - i) // 2

        @pl.when(i % 2 == 0)
        def _():
            for h in range(GROUP):
                out[g, :, h * HEAD : (h + 1) * HEAD] = values(h).astype(BF)
            to_sibling(out, sib, sib_send, sib_recv, g, j).start()

        @pl.when(i % 2 == 1)
        def _():
            to_sibling(out, sib, sib_send, sib_recv, g, j).wait_recv()
            for h in range(GROUP):
                cols = slice(h * HEAD, (h + 1) * HEAD)
                out[g, :, cols] = (values(h) + sib[j, :, cols].astype(F32)).astype(BF)

        @pl.when((i % 2 == 1) & (i < groups - 1))
        def _():
            to_owner(out, dest, send, recv, g, j).start()

    def settle(out, dest, recv, send, n):
        for j in range(1, chips):
            src = (z + j) % chips
            remote(out.at[0], dest.at[src], send.at[0], recv.at[src], (row, 2 * src + core)).wait_recv()
        dest[z] = out[me]
        for h in range(GROUP):
            cols = slice(h * HEAD, (h + 1) * HEAD)
            sums = []
            for i in range(2):
                sums.append(dest[2 * i, :, cols].astype(F32) + dest[2 * i + 1, :, cols].astype(F32))
            kept = [jnp.where(own_rows[i], sums[i], 0.0) for i in range(2)]
            gone = [jnp.where(own_rows[i], 0.0, sums[i]) for i in range(2)]
            stay[n, :, cols] = kept[0] + kept[1]
            leave[n, :, cols] = (gone[0] + gone[1]).astype(BF)
            if h % PIECE == PIECE - 1:
                leave_copy(n, h // PIECE).start()

    def leave_copy(n, k):
        cols = slice(k * PIECE * HEAD, (k + 1) * PIECE * HEAD)
        sem = n * (GROUP // PIECE) + k
        return remote(
            leave.at[n, :, cols], arrived.at[n, :, cols], leave_send.at[sem], leave_recv.at[sem], (above, me)
        )

    def backward(i, carry):
        g = group_at(groups - 1 - i)
        slot = i % 2
        kv_load(g, slot).wait()

        @pl.when(i < groups - 1)
        def _():
            kv_load(group_at(groups - 2 - i), 1 - slot).start()
            remote(fin_out.at[0], fin_in.at[g], fin_send.at[0], fin_recv.at[g], (row, g)).wait_recv()

        lse, mean = fin_in[g, 0], fin_in[g, 1]
        weight[0] = jnp.where(shown, jnp.exp2(tops[g] - lse), 0.0)
        weight[1] = jnp.where(shown, jnp.exp2(stat_out[g, 0] - lse), 0.0)
        weight[2] = mean

        def lanes_of(n):
            return jnp.concatenate([weight[n, h : h + 1, :] for h in range(GROUP)], 1)

        def o_rows(h):
            return (out_t[g, :, h * SLOTS : (h + 1) * SLOTS] * weight[1, h : h + 1, :]).T

        pass_on(o_rows, o_out, o_sib, o_in, o_sib_send, o_sib_recv, o_send, o_recv, i, g)

        @pl.when(i == groups - 1)
        def _():
            settle(o_out, o_in, o_recv, o_send, 0)

        @pl.when(i >= 2)
        def _():
            dkv_store(g, slot).wait()

        split_tile(keys, kv_buf[slot, 0:keys], wide, k_pad, v_pad)
        turned[...] = k_pad[...].T
        backward_group(
            keys,
            v_pad,
            turned,
            head_rows(q_all[g]),
            head_rows(g_all[g]),
            probs.at[g],
            lanes_of(0),
            lanes_of(2),
            dq_t,
            wide,
        )
        def d_rows(h):
            return (dq_t[:, h * SLOTS : (h + 1) * SLOTS] * SCALE).T

        pass_on(d_rows, d_out, d_sib, d_in, d_sib_send, d_sib_recv, d_send, d_recv, i, g)
        dkv_buf[slot, 0:keys] = wide[0 : 2 * keys, :].astype(BF).reshape(keys, 2, HEAD)
        dkv_store(g, slot).start()
        return carry

    lax.fori_loop(0, groups, backward, 0)
    settle(d_out, d_in, d_recv, d_send, 1)

    for n, result in enumerate((attended_ref, dq_ref)):
        for h in range(GROUP):
            if h % PIECE == 0:
                leave_copy(n, h // PIECE).wait_recv()
            cols = slice(h * HEAD, (h + 1) * HEAD)
            total = stay[n, :, cols] + arrived[n, :, cols].astype(F32)
            result[:, cols] = (gate * total if n == 0 else total).astype(BF)

    send_q.wait_send()
    send_g.wait_send()
    for n in range(7):
        hand_on(q_all, q_send, q_recv, 2, n).wait_send()
        hand_on(g_all, g_send, g_recv, 2, n).wait_send()
    for n in range(1, groups):
        stat_copy(0, n).wait_send()
        remote(fin_out.at[0], fin_in.at[0], fin_send.at[n], fin_recv.at[0], (row, other)).wait_send()
    for j in range(chips):
        to_sibling(o_out, o_sib, o_sib_send, o_sib_recv, 0, j).wait_send()
        to_sibling(d_out, d_sib, d_sib_send, d_sib_recv, 0, j).wait_send()
    for j in range(1, chips):
        remote(o_out.at[0], o_in.at[0], o_send.at[j], o_recv.at[0], (row, other)).wait_send()
        remote(d_out.at[0], d_in.at[0], d_send.at[j], d_recv.at[0], (row, other)).wait_send()
    up.wait_send()
    down.wait_send()
    for n in range(2):
        for k in range(GROUP // PIECE):
            leave_copy(n, k).wait_send()
        dkv_store(0, n).wait()


def finish_kernel(pieces, a_in, d_in, kv_in, a_out, d_out, kv_out, a_buf, d_buf, kv_buf, loads, stores):
    keys = kv_in.shape[0]
    step = -(-keys // pieces)
    parts = [slice(n * step, min((n + 1) * step, keys)) for n in range(pieces)]
    moves = [(a_in, a_buf, a_out), (d_in, d_buf, d_out)]
    moves += [(kv_in.at[p], kv_buf.at[p], kv_out.at[p]) for p in parts]
    into = [pltpu.make_async_copy(m[0], m[1], loads.at[n]) for n, m in enumerate(moves)]
    out = [pltpu.make_async_copy(m[1], m[2], stores.at[n]) for n, m in enumerate(moves)]
    for copy in into:
        copy.start()
    for copy, store in zip(into, out):
        copy.wait()
        store.start()
    for store in out:
        store.wait()


def shards(queries, image_key_value, image_spans, tile_counts, cross_gate, grad_out):
    groups = lax.axis_size("enc")
    keys = image_key_value.shape[2]
    padded = chunks(keys, 896)[0]
    kv = image_key_value.reshape(2, keys, groups, HEAD).transpose(1, 2, 0, 3)
    wide = GROUP * HEAD
    vmem = pl.BlockSpec(memory_space=pltpu.VMEM)
    smem = pl.BlockSpec(memory_space=pltpu.SMEM)
    anywhere = pl.BlockSpec(memory_space=pl.ANY)
    block = pltpu.VMEM((SLOTS, wide), BF)
    pair = pltpu.VMEM((2, SLOTS, wide), BF)
    every = pltpu.VMEM((groups, SLOTS, wide), BF)
    quarter = pltpu.VMEM((groups // 2, SLOTS, wide), BF)
    stats = pltpu.VMEM((groups, 2, GROUP, SLOTS), F32)
    two_stats = pltpu.VMEM((2, 2, GROUP, SLOTS), F32)
    text = jax.ShapeDtypeStruct((SLOTS, wide), BF)
    sems = [2, 2, 2, 2, 2, 7, 8, 7, 8, 8, 8, 2, 2, 8, 8] + [4] * 8 + [8, 8]
    attended, grad_queries, dkv = pl.pallas_call(
        functools.partial(step_kernel, keys),
        out_shape=[text, text, jax.ShapeDtypeStruct(kv.shape, BF)],
        in_specs=[anywhere, anywhere, anywhere, smem, smem, smem],
        out_specs=[vmem, vmem, anywhere],
        scratch_shapes=[
            block,
            block,
            block,
            block,
            block,
            pair,
            pair,
            every,
            every,
            pltpu.VMEM((2, padded, 2, HEAD), BF),
            pltpu.VMEM((2, padded, 2, HEAD), BF),
            pltpu.VMEM((2 * padded, HEAD), F32),
            pltpu.VMEM((padded, HEAD), BF),
            pltpu.VMEM((padded, HEAD), BF),
            pltpu.VMEM((HEAD, padded), BF),
            pltpu.VMEM((padded, ROWS), F32),
            pltpu.VMEM((groups, padded, ROWS), BF),
            pltpu.VMEM((groups, HEAD, ROWS), F32),
            pltpu.VMEM((HEAD, ROWS), F32),
            pltpu.VMEM((groups, GROUP, SLOTS), F32),
            stats,
            stats,
            two_stats,
            two_stats,
            two_stats,
            stats,
            pltpu.VMEM((3, GROUP, SLOTS), F32),
            every,
            quarter,
            quarter,
            every,
            quarter,
            quarter,
            pltpu.VMEM((2, SLOTS, wide), F32),
            pair,
            pair,
        ]
        + [pltpu.SemaphoreType.DMA((n,)) for n in sems],
        compiler_params=pltpu.CompilerParams(
            collective_id=0, has_side_effects=True, vmem_limit_bytes=63 * 2**20
        ),
    )(queries, grad_out, kv, image_spans.T, tile_counts, cross_gate)
    pieces = 16
    attended, grad_queries, dkv = pl.pallas_call(
        functools.partial(finish_kernel, pieces),
        out_shape=[text, text, jax.ShapeDtypeStruct(kv.shape, BF)],
        in_specs=[anywhere] * 3,
        out_specs=[anywhere] * 3,
        scratch_shapes=[block, block, pltpu.VMEM(kv.shape, BF)]
        + [pltpu.SemaphoreType.DMA((pieces + 2,))] * 2,
        compiler_params=pltpu.CompilerParams(vmem_limit_bytes=62 * 2**20),
    )(attended, grad_queries, dkv)
    grad_image_kv = dkv.transpose(2, 0, 1, 3).reshape(2, 1, keys, groups * HEAD)
    return attended, grad_queries, grad_image_kv


def solution(mesh):
    kv_part = P(None, ("seq", "enc"), None, None)
    return jax.shard_map(
        shards,
        mesh=mesh,
        in_specs=(P("seq", "enc"), kv_part, P(), P(), P(), P("seq", "enc")),
        out_specs=(P("seq", "enc"), P("seq", "enc"), kv_part),
        check_vma=False,
    )
```

```python
import functools

import jax
import jax.numpy as jnp
from jax import lax
from jax.experimental import pallas as pl
from jax.experimental.pallas import tpu as pltpu
from jax.sharding import PartitionSpec as P

HEAD = 128
SLOTS = 128
TILES = 4
GROUP = 8
ROWS = GROUP * SLOTS
NEG = -1e30
LOG2E = 1.4426950408889634
SCALE = HEAD**-0.5
NT = (((1,), (1,)), ((), ()))
NN = (((1,), (0,)), ((), ()))
BF = jnp.bfloat16
F32 = jnp.float32


def dot(a, b, dims=NN):
    return lax.dot_general(a, b, dims, preferred_element_type=F32)


def chunks(keys, size):
    padded = -(-keys // 128) * 128
    return padded, [(o, min(size, padded - o)) for o in range(0, padded, size)]


def head_rows(block):
    return jnp.concatenate([block[:, h * HEAD : (h + 1) * HEAD] for h in range(GROUP)], 0)


def split_tile(keys, kv_block, wide, k_pad, v_pad):
    padded = k_pad.shape[0]
    wide[0 : 2 * keys, :] = kv_block.reshape(2 * keys, HEAD).astype(F32)
    wide[2 * keys :, :] = jnp.zeros((2 * (padded - keys), HEAD), F32)
    k_pad[...] = wide[pl.ds(0, padded, 2), :].astype(BF)
    v_pad[...] = wide[pl.ds(1, padded, 2), :].astype(BF)


def forward_group(keys, k_pad, v_t, q, probs, scores, out_t):
    padded, parts = chunks(keys, 256)
    top = jnp.full((8, ROWS), NEG, F32)
    for o, n in parts:
        s = dot(k_pad[o : o + n, :], q, NT)
        if o + n > keys:
            s = jnp.where(lax.broadcasted_iota(jnp.int32, s.shape, 0) < keys - o, s, NEG)
        scores[o : o + n, :] = s
        top = jnp.maximum(top, jnp.max(s.reshape(n // 8, 8, ROWS), axis=0))
    top = jnp.max(top, axis=0, keepdims=True) * (SCALE * LOG2E)
    total = jnp.zeros((8, ROWS), F32)
    acc = jnp.zeros((HEAD, ROWS), F32)
    for o, n in parts:
        p = jnp.exp2(scores[o : o + n, :] * (SCALE * LOG2E) - top)
        total = total + jnp.sum(p.reshape(n // 8, 8, ROWS), axis=0)
        low = p.astype(BF)
        probs[o : o + n, :] = low
        acc = acc + dot(v_t[:, o : o + n], low)
    total = jnp.sum(total, axis=0, keepdims=True)
    out_t[...] = acc / total
    return top, top + jnp.log2(total)


def backward_group(keys, v_pad, k_t, q, g, probs, factor, delta, dq_t, wide):
    padded, parts = chunks(keys, 256)
    for o, n in parts:
        dp = dot(v_pad[o : o + n, :], g, NT)
        p = probs[o : o + n, :].astype(F32) * factor
        t = (p * (dp - delta)).astype(BF)
        wide[pl.ds(2 * o, n, 2), :] = dot(t, q) * SCALE
        wide[pl.ds(2 * o + 1, n, 2), :] = dot(p.astype(BF), g)
        d = dot(k_t[:, o : o + n], t)
        dq_t[...] = d if o == 0 else dq_t[...] + d


MESH = pl.DeviceIdType.MESH
LAG = 3


def merged(entries):
    top = entries[0][0]
    for lse, _ in entries[1:]:
        top = jnp.maximum(top, lse)
    total = jnp.zeros_like(top)
    mean = jnp.zeros_like(top)
    for lse, delta in entries:
        part = jnp.where(lse > 0.5 * NEG, jnp.exp2(lse - top), 0.0)
        total = total + part
        mean = mean + part * delta
    seen = total > 0.0
    safe = jnp.where(seen, total, 1.0)
    return jnp.where(seen, top + jnp.log2(safe), NEG), mean / safe


def step_kernel(
    keys,
    q_hbm,
    g_hbm,
    kv_ref,
    spans,
    counts,
    gate_ref,
    attended_ref,
    dq_ref,
    dkv_ref,
    q_ref,
    g_ref,
    g_low,
    next_q,
    next_g,
    pick_q,
    pick_g,
    q_all,
    g_all,
    kv_buf,
    dkv_buf,
    wide,
    k_pad,
    v_pad,
    turned,
    scores,
    probs,
    out_t,
    dq_t,
    tops,
    stat_out,
    stat_in,
    seq_out,
    seq_in,
    fin_out,
    fin_in,
    weight,
    o_out,
    o_sib,
    o_in,
    d_out,
    d_sib,
    d_in,
    stay,
    leave,
    arrived,
    text_sem,
    kv_sem,
    dkv_sem,
    next_send,
    next_recv,
    q_send,
    q_recv,
    g_send,
    g_recv,
    stat_send,
    stat_recv,
    seq_send,
    seq_recv,
    fin_send,
    fin_recv,
    o_sib_send,
    o_sib_recv,
    o_send,
    o_recv,
    d_sib_send,
    d_sib_recv,
    d_send,
    d_recv,
    leave_send,
    leave_recv,
):
    row = lax.axis_index("seq")
    me = lax.axis_index("enc")
    rows = lax.axis_size("seq")
    groups = lax.axis_size("enc")
    chips = groups // 2
    z, core = me // 2, me % 2
    other = me + 1 - 2 * core
    image = me // TILES
    above, below = (row + 1) % rows, (row + rows - 1) % rows

    def remote(src, dst, send, recv, to):
        return pltpu.make_async_remote_copy(
            src_ref=src, dst_ref=dst, send_sem=send, recv_sem=recv, device_id=to, device_id_type=MESH
        )

    def group_at(i):
        j = i // 2
        hop = j + j // 2 - 2 * (j // 3)
        return 2 * ((z + hop) % chips) + (core + i) % 2

    def kv_load(g, slot):
        return pltpu.make_async_copy(kv_ref.at[:, g], kv_buf.at[slot, 0:keys], kv_sem.at[slot])

    def dkv_store(g, slot):
        return pltpu.make_async_copy(dkv_buf.at[slot, 0:keys], dkv_ref.at[:, g], dkv_sem.at[slot])

    text = [
        pltpu.make_async_copy(q_hbm, q_ref, text_sem.at[0]),
        pltpu.make_async_copy(g_hbm, g_ref, text_sem.at[1]),
    ]
    for copy in text:
        copy.start()
    kv_load(group_at(0), 0).start()

    barrier = pltpu.get_barrier_semaphore()
    for j in range(1, groups):
        pl.semaphore_signal(barrier, inc=1, device_id=(row, (me + j) % groups), device_id_type=MESH)
    for r in (above, below):
        pl.semaphore_signal(barrier, inc=1, device_id=(r, me), device_id_type=MESH)
    pl.semaphore_wait(barrier, groups + 1)

    to_below = (below, me)
    text[0].wait()
    send_q = remote(q_ref, next_q, next_send.at[0], next_recv.at[0], to_below)
    send_q.start()
    text[1].wait()
    gate = jnp.tanh(jnp.full((SLOTS, HEAD), gate_ref[0], F32))
    for h in range(GROUP):
        cols = slice(h * HEAD, (h + 1) * HEAD)
        g_low[:, cols] = (gate * g_ref[:, cols].astype(F32)).astype(BF)
    send_g = remote(g_low, next_g, next_send.at[1], next_recv.at[1], to_below)
    send_g.start()

    starts = [spans[0, 2 * row + i] for i in range(2)]
    ends = [spans[1, 2 * row + i] for i in range(2)]
    used = [counts[2 * row + i] for i in range(2)]
    at_rows = row * SLOTS + lax.broadcasted_iota(jnp.int32, (SLOTS, HEAD), 0)
    at_lanes = row * SLOTS + lax.broadcasted_iota(jnp.int32, (GROUP, SLOTS), 1)
    own_rows = [at_rows >= starts[i] for i in range(2)]
    own_lanes = [at_lanes >= starts[i] for i in range(2)]

    def fan_out(mine, later, picked, everywhere, send, recv):
        for h in range(GROUP):
            cols = slice(h * HEAD, (h + 1) * HEAD)
            a, b = mine[:, cols].astype(F32), later[:, cols].astype(F32)
            for i in range(2):
                picked[i, :, cols] = jnp.where(own_rows[i], a, b).astype(BF)
        everywhere[me] = picked[image]
        remote(picked.at[image], everywhere.at[me], send.at[0], recv.at[me], (row, other)).start()
        for n, hop in enumerate((1, chips - 1, 2)):
            peer = 2 * ((z + hop) % chips) + core
            remote(
                picked.at[peer // TILES], everywhere.at[me], send.at[1 + n], recv.at[me], (row, peer)
            ).start()

    def arrival(buf, send, recv, g):
        return remote(buf.at[g], buf.at[g], send.at[0], recv.at[g], (row, other))

    def hand_on(buf, send, recv, i, n):
        g = group_at(i)
        return remote(buf.at[g], buf.at[g], send.at[n], recv.at[g], (row, other))

    send_q.wait_recv()
    fan_out(q_ref, next_q, pick_q, q_all, q_send, q_recv)

    def stat_copy(g, n):
        return remote(stat_out.at[g], stat_in.at[me], stat_send.at[n], stat_recv.at[me], (row, g))

    def delta(g):
        for h in range(GROUP):
            lanes = slice(h * SLOTS, (h + 1) * SLOTS)
            g_t = g_all[g, :, h * HEAD : (h + 1) * HEAD].T.astype(F32)
            stat_out[g, 1, h : h + 1, :] = jnp.sum(out_t[g, :, lanes] * g_t, axis=0, keepdims=True)

    def forward(i, carry):
        g = group_at(i)
        slot = i % 2
        kv_load(g, slot).wait()
        kv_load(group_at(jnp.minimum(i + 1, groups - 1)), 1 - slot).start()

        @pl.when(i > 0)
        def _():
            arrival(q_all, q_send, q_recv, g).wait_recv()

        @pl.when(i == 1)
        def _():
            send_g.wait_recv()
            fan_out(g_low, next_g, pick_g, g_all, g_send, g_recv)

        for n in range(3):

            @pl.when(i == 2 + 2 * n)
            def _():
                hand_on(q_all, q_send, q_recv, 2 + 2 * n, 4 + n).start()

            @pl.when(i == 5 + n)
            def _():
                arrival(g_all, g_send, g_recv, group_at(2 + 2 * n)).wait_recv()
                hand_on(g_all, g_send, g_recv, 2 + 2 * n, 4 + n).start()

        late = group_at(jnp.maximum(i - LAG, 0))

        @pl.when((i > LAG) & ((i - LAG) % 2 == 1))
        def _():
            arrival(g_all, g_send, g_recv, late).wait_recv()

        delta(late)

        @pl.when(i > LAG)
        def _():
            stat_copy(late, i - LAG).start()

        split_tile(keys, kv_buf[slot, 0:keys], wide, k_pad, v_pad)
        turned[...] = v_pad[...].T
        top, lse = forward_group(
            keys, k_pad, turned, head_rows(q_all[g]), probs.at[g], scores, out_t.at[g]
        )
        for h in range(GROUP):
            lanes = slice(h * SLOTS, (h + 1) * SLOTS)
            tops[g, h : h + 1, :] = top[:, lanes]
            stat_out[g, 0, h : h + 1, :] = lse[:, lanes]
        return carry

    lax.fori_loop(0, groups, forward, 0)

    for i in range(TILES * 2 - LAG, TILES * 2):
        late = group_at(i)
        if i % 2 == 1:
            arrival(g_all, g_send, g_recv, late).wait_recv()
        delta(late)
        stat_copy(late, i).start()
    stat_in[me] = stat_out[me]
    for j in range(1, groups):
        src = (me + j) % groups
        remote(stat_out.at[0], stat_in.at[src], stat_send.at[0], stat_recv.at[src], (row, src)).wait_recv()

    def seen(c, shift):
        i = c // TILES
        end = jnp.where(c % TILES < used[i], ends[i], 0)
        at = at_lanes + shift
        return (at >= starts[i]) & (at < end)

    here, after = [], []
    for c in range(2 * TILES):
        lse, mean = stat_in[c, 0], stat_in[c, 1]
        here.append((jnp.where(seen(c, 0), lse, NEG), mean))
        after.append((jnp.where(seen(c, SLOTS), lse, NEG), mean))
    here, after = merged(here), merged(after)
    seq_out[0, 0], seq_out[0, 1] = after
    seq_out[1, 0], seq_out[1, 1] = here
    up = remote(seq_out.at[0], seq_in.at[0], seq_send.at[0], seq_recv.at[0], (above, me))
    down = remote(seq_out.at[1], seq_in.at[1], seq_send.at[1], seq_recv.at[1], (below, me))
    up.start()
    down.start()
    up.wait_recv()
    down.wait_recv()
    here = merged([here, (seq_in[0, 0], seq_in[0, 1])])
    after = merged([after, (seq_in[1, 0], seq_in[1, 1])])
    for i in range(2):
        for n in range(2):
            fin_out[i, n] = jnp.where(own_lanes[i], here[n], after[n])
    fin_in[me] = fin_out[image]
    for j in range(1, groups):
        c = (me + j) % groups
        remote(fin_out.at[c // TILES], fin_in.at[me], fin_send.at[j], fin_recv.at[me], (row, c)).start()

    my_used = counts[2 * row + image]
    my_start = spans[0, 2 * row + image]
    my_end = jnp.where(me % TILES < my_used, spans[1, 2 * row + image], 0)
    shown = ((at_lanes >= my_start) & (at_lanes < my_end)) | (
        (at_lanes + SLOTS >= my_start) & (at_lanes + SLOTS < my_end)
    )

    def to_sibling(out, sib, send, recv, g, j):
        return remote(out.at[g], sib.at[j], send.at[j], recv.at[j], (row, other))

    def to_owner(out, dest, send, recv, g, j):
        return remote(out.at[g], dest.at[z], send.at[j], recv.at[z], (row, g))

    def pass_on(values, out, sib, dest, sib_send, sib_recv, send, recv, i, g):
        j = (groups - 1 - i) // 2

        @pl.when(i % 2 == 0)
        def _():
            for h in range(GROUP):
                out[g, :, h * HEAD : (h + 1) * HEAD] = values(h).astype(BF)
            to_sibling(out, sib, sib_send, sib_recv, g, j).start()

        @pl.when(i % 2 == 1)
        def _():
            to_sibling(out, sib, sib_send, sib_recv, g, j).wait_recv()
            for h in range(GROUP):
                cols = slice(h * HEAD, (h + 1) * HEAD)
                out[g, :, cols] = (values(h) + sib[j, :, cols].astype(F32)).astype(BF)

        @pl.when((i % 2 == 1) & (i < groups - 1))
        def _():
            to_owner(out, dest, send, recv, g, j).start()

    def settle(out, dest, recv, send, n):
        for j in range(1, chips):
            src = (z + j) % chips
            remote(out.at[0], dest.at[src], send.at[0], recv.at[src], (row, 2 * src + core)).wait_recv()
        dest[z] = out[me]
        for h in range(GROUP):
            cols = slice(h * HEAD, (h + 1) * HEAD)
            sums = []
            for i in range(2):
                sums.append(dest[2 * i, :, cols].astype(F32) + dest[2 * i + 1, :, cols].astype(F32))
            kept = [jnp.where(own_rows[i], sums[i], 0.0) for i in range(2)]
            gone = [jnp.where(own_rows[i], 0.0, sums[i]) for i in range(2)]
            stay[n, :, cols] = kept[0] + kept[1]
            leave[n, :, cols] = (gone[0] + gone[1]).astype(BF)
        leave_copy(n).start()

    def leave_copy(n):
        return remote(leave.at[n], arrived.at[n], leave_send.at[n], leave_recv.at[n], (above, me))

    def backward(i, carry):
        g = group_at(groups - 1 - i)
        slot = i % 2
        kv_load(g, slot).wait()

        split_tile(keys, kv_buf[slot, 0:keys], wide, k_pad, v_pad)
        turned[...] = k_pad[...].T

        @pl.when(i < groups - 1)
        def _():
            kv_load(group_at(groups - 2 - i), 1 - slot).start()
            remote(fin_out.at[0], fin_in.at[g], fin_send.at[0], fin_recv.at[g], (row, g)).wait_recv()

        lse, mean = fin_in[g, 0], fin_in[g, 1]
        weight[0] = jnp.where(shown, jnp.exp2(tops[g] - lse), 0.0)
        weight[1] = jnp.where(shown, jnp.exp2(stat_out[g, 0] - lse), 0.0)
        weight[2] = mean

        def lanes_of(n):
            return jnp.concatenate([weight[n, h : h + 1, :] for h in range(GROUP)], 1)

        def o_rows(h):
            return (out_t[g, :, h * SLOTS : (h + 1) * SLOTS] * weight[1, h : h + 1, :]).T

        pass_on(o_rows, o_out, o_sib, o_in, o_sib_send, o_sib_recv, o_send, o_recv, i, g)

        @pl.when(i == groups - 1)
        def _():
            settle(o_out, o_in, o_recv, o_send, 0)

        @pl.when(i >= 2)
        def _():
            dkv_store(g, slot).wait()

        backward_group(
            keys,
            v_pad,
            turned,
            head_rows(q_all[g]),
            head_rows(g_all[g]),
            probs.at[g],
            lanes_of(0),
            lanes_of(2),
            dq_t,
            wide,
        )
        def d_rows(h):
            return (dq_t[:, h * SLOTS : (h + 1) * SLOTS] * SCALE).T

        pass_on(d_rows, d_out, d_sib, d_in, d_sib_send, d_sib_recv, d_send, d_recv, i, g)
        dkv_buf[slot, 0:keys] = wide[0 : 2 * keys, :].astype(BF).reshape(keys, 2, HEAD)
        dkv_store(g, slot).start()
        return carry

    lax.fori_loop(0, groups, backward, 0)
    settle(d_out, d_in, d_recv, d_send, 1)

    for n, result in enumerate((attended_ref, dq_ref)):
        leave_copy(n).wait_recv()
        for h in range(GROUP):
            cols = slice(h * HEAD, (h + 1) * HEAD)
            total = stay[n, :, cols] + arrived[n, :, cols].astype(F32)
            result[:, cols] = (gate * total if n == 0 else total).astype(BF)

    send_q.wait_send()
    send_g.wait_send()
    for n in range(7):
        hand_on(q_all, q_send, q_recv, 2, n).wait_send()
        hand_on(g_all, g_send, g_recv, 2, n).wait_send()
    for n in range(1, groups):
        stat_copy(0, n).wait_send()
        remote(fin_out.at[0], fin_in.at[0], fin_send.at[n], fin_recv.at[0], (row, other)).wait_send()
    for j in range(chips):
        to_sibling(o_out, o_sib, o_sib_send, o_sib_recv, 0, j).wait_send()
        to_sibling(d_out, d_sib, d_sib_send, d_sib_recv, 0, j).wait_send()
    for j in range(1, chips):
        remote(o_out.at[0], o_in.at[0], o_send.at[j], o_recv.at[0], (row, other)).wait_send()
        remote(d_out.at[0], d_in.at[0], d_send.at[j], d_recv.at[0], (row, other)).wait_send()
    up.wait_send()
    down.wait_send()
    for n in range(2):
        leave_copy(n).wait_send()
        dkv_store(0, n).wait()


def finish_kernel(pieces, a_in, d_in, kv_in, a_out, d_out, kv_out, a_buf, d_buf, kv_buf, loads, stores):
    keys = kv_in.shape[0]
    step = -(-keys // pieces)
    parts = [slice(n * step, min((n + 1) * step, keys)) for n in range(pieces)]
    moves = [(a_in, a_buf, a_out), (d_in, d_buf, d_out)]
    moves += [(kv_in.at[p], kv_buf.at[p], kv_out.at[p]) for p in parts]
    into = [pltpu.make_async_copy(m[0], m[1], loads.at[n]) for n, m in enumerate(moves)]
    out = [pltpu.make_async_copy(m[1], m[2], stores.at[n]) for n, m in enumerate(moves)]
    for copy in into:
        copy.start()
    for copy, store in zip(into, out):
        copy.wait()
        store.start()
    for store in out:
        store.wait()


def shards(queries, image_key_value, image_spans, tile_counts, cross_gate, grad_out):
    groups = lax.axis_size("enc")
    keys = image_key_value.shape[2]
    padded = chunks(keys, 256)[0]
    kv = image_key_value.reshape(2, keys, groups, HEAD).transpose(1, 2, 0, 3)
    wide = GROUP * HEAD
    vmem = pl.BlockSpec(memory_space=pltpu.VMEM)
    smem = pl.BlockSpec(memory_space=pltpu.SMEM)
    anywhere = pl.BlockSpec(memory_space=pl.ANY)
    block = pltpu.VMEM((SLOTS, wide), BF)
    pair = pltpu.VMEM((2, SLOTS, wide), BF)
    every = pltpu.VMEM((groups, SLOTS, wide), BF)
    quarter = pltpu.VMEM((groups // 2, SLOTS, wide), BF)
    stats = pltpu.VMEM((groups, 2, GROUP, SLOTS), F32)
    two_stats = pltpu.VMEM((2, 2, GROUP, SLOTS), F32)
    text = jax.ShapeDtypeStruct((SLOTS, wide), BF)
    sems = [2, 2, 2, 2, 2, 7, 8, 7, 8, 8, 8, 2, 2, 8, 8] + [4] * 8 + [2, 2]
    attended, grad_queries, dkv = pl.pallas_call(
        functools.partial(step_kernel, keys),
        out_shape=[text, text, jax.ShapeDtypeStruct(kv.shape, BF)],
        in_specs=[anywhere, anywhere, anywhere, smem, smem, smem],
        out_specs=[vmem, vmem, anywhere],
        scratch_shapes=[
            block,
            block,
            block,
            block,
            block,
            pair,
            pair,
            every,
            every,
            pltpu.VMEM((2, padded, 2, HEAD), BF),
            pltpu.VMEM((2, padded, 2, HEAD), BF),
            pltpu.VMEM((2 * padded, HEAD), F32),
            pltpu.VMEM((padded, HEAD), BF),
            pltpu.VMEM((padded, HEAD), BF),
            pltpu.VMEM((HEAD, padded), BF),
            pltpu.VMEM((padded, ROWS), F32),
            pltpu.VMEM((groups, padded, ROWS), BF),
            pltpu.VMEM((groups, HEAD, ROWS), F32),
            pltpu.VMEM((HEAD, ROWS), F32),
            pltpu.VMEM((groups, GROUP, SLOTS), F32),
            stats,
            stats,
            two_stats,
            two_stats,
            two_stats,
            stats,
            pltpu.VMEM((3, GROUP, SLOTS), F32),
            every,
            quarter,
            quarter,
            every,
            quarter,
            quarter,
            pltpu.VMEM((2, SLOTS, wide), F32),
            pair,
            pair,
        ]
        + [pltpu.SemaphoreType.DMA((n,)) for n in sems],
        compiler_params=pltpu.CompilerParams(
            collective_id=0, has_side_effects=True, vmem_limit_bytes=63 * 2**20
        ),
    )(queries, grad_out, kv, image_spans.T, tile_counts, cross_gate)
    pieces = 16
    attended, grad_queries, dkv = pl.pallas_call(
        functools.partial(finish_kernel, pieces),
        out_shape=[text, text, jax.ShapeDtypeStruct(kv.shape, BF)],
        in_specs=[anywhere] * 3,
        out_specs=[anywhere] * 3,
        scratch_shapes=[block, block, pltpu.VMEM(kv.shape, BF)]
        + [pltpu.SemaphoreType.DMA((pieces + 2,))] * 2,
        compiler_params=pltpu.CompilerParams(vmem_limit_bytes=62 * 2**20),
    )(attended, grad_queries, dkv)
    grad_image_kv = dkv.transpose(2, 0, 1, 3).reshape(2, 1, keys, groups * HEAD)
    return attended, grad_queries, grad_image_kv


def solution(mesh):
    kv_part = P(None, ("seq", "enc"), None, None)
    return jax.shard_map(
        shards,
        mesh=mesh,
        in_specs=(P("seq", "enc"), kv_part, P(), P(), P(), P("seq", "enc")),
        out_specs=(P("seq", "enc"), P("seq", "enc"), kv_part),
        check_vma=False,
    )
```
